32 devices in a mesh: row: 2 (over x), col: 8 (over z, core), freq: 2 (over y).
Axes of the slice: x: 2, y: 2, z: 4, core: 2. Of those that a mesh axis runs over, the one named last changes fastest.
Arguments:
- left_data: float32 [2, 2048, 512], P(None, ('freq', 'row'), 'col'), parts along dimension 1, may hold values from -6 to 6
- right_data: float32 [2, 512, 8192], P(None, 'row', ('freq', 'col')), parts along dimension 2, may hold values from -0.1875 to 0.1875
Outputs:
- multiples: float32 [2, 2048, 4096], P(None, ('freq', 'row'), 'col'), parts along dimension 1
The draws below stay inside these ranges and needn't reach their ends.
There are 2 independent parts, one for each index of `freq`. The reference program is written for one: setup_inputs(seed, part) draws one part's arguments, and reference() takes and returns one part's arrays. A program takes and returns all parts, laid end to end along the dimension named above; each array names one. Nothing has to cross between parts.
All inputs are finite; a program needn't handle non-finite values.
Results may differ from the reference program's by a relative error of at most 0.000071.
Values sent between devices are 32-bit elements; how exact they have to be, the bound alone decides.
A program may use at most 64 MiB of HBM per device.

```python
import jax
import jax.numpy as jnp
from jax import lax

KW = 512
MR = 1024
MC = 4096


def level_of(own_key, extent, pieces, least, high):
    gain, own = 1.0, jax.random.fold_in(own_key, 6)
    for dim, shards_of in pieces:
        steps = jnp.exp(jax.random.uniform(jax.random.fold_in(own, dim), (shards_of,), jnp.float32, least / len(pieces), high / len(pieces)))
        gain = gain * jnp.repeat(steps, extent[dim] // shards_of).reshape([-1 if axis == dim else 1 for axis in range(len(extent))])
    return gain


def scatter_about(own_key, shape, deviation, most, pieces=(), dtype=jnp.bfloat16):
    drawn = deviation * jax.random.normal(own_key, shape, jnp.float32)
    if pieces:
        drawn = drawn * level_of(own_key, shape, pieces, -0.22, 0.18)
    return jnp.clip(drawn, -most, most).astype(dtype)


def setup_inputs(seed: int = 0, part: int = 0) -> dict:
    key_list = jax.random.split(jax.random.key(seed), 3)
    own_keys = jax.random.split(jax.random.fold_in(key_list[2], part), 3)
    left_data = scatter_about(own_keys[0], (2, MR, KW), 1.0, 6.0, ((1, 2), (2, 8)), jnp.float32)
    right_data = scatter_about(own_keys[1], (2, KW, MC), (2 * KW) ** -0.5, 0.1875, ((1, 2), (2, 8)), jnp.float32)
    return dict(left_data=left_data, right_data=right_data)


def matmul_hi(a, b):
    return jnp.dot(a, b, preferred_element_type=jnp.float32, precision=lax.Precision.HIGHEST)


def reference(left_data, right_data):
    real_part = matmul_hi(left_data[0], right_data[0]) - matmul_hi(left_data[1], right_data[1])
    imag_part = matmul_hi(left_data[0], right_data[1]) + matmul_hi(left_data[1], right_data[0])
    return jnp.stack([real_part, imag_part], axis=0)
```

```python
import functools

import jax
import jax.numpy as jnp
from jax import lax
from jax.experimental import pallas as pl
from jax.experimental.pallas import tpu as pltpu
from jax.sharding import PartitionSpec as P

MESH = pl.DeviceIdType.MESH
LANES = 128
PAIR = 2 * LANES


def split(value):
    high = value.astype(jnp.bfloat16)
    return high, (value - high.astype(jnp.float32)).astype(jnp.bfloat16)


def dot(a, b):
    return jnp.dot(a, b, preferred_element_type=jnp.float32)


def three_dots(left_hi, left_lo, w_hi, w_lo):
    return dot(left_hi, w_hi) + (dot(left_hi, w_lo) + dot(left_lo, w_hi))


def by_slab(kb, kr, line):
    return 2 * kb == LANES and kr % LANES == 0 and line > 1


def right_pieces(kb, kr, line, chunks):
    pieces = [(j, 0, kr) for j in range(chunks)]
    if by_slab(kb, kr, line):
        pieces[-1:] = [(chunks - 1, r, LANES) for r in range(0, kr, LANES)]
    return pieces


def write(done_ref, out_hbm, sem):
    copy = pltpu.make_async_copy(done_ref, out_hbm, sem.at[0])
    copy.start()
    copy.wait()


def kernel(
    n_row, n_col, left_hbm, right_hbm, out_ref, left_hi, left_lo, w_hi, w_lo,
    left_f32, right_f32, own_sem, near, left_send, left_recv, right_send, right_recv,
):
    _, kb, rows = left_hbm.shape
    _, kr, cols = right_hbm.shape
    depth = kb * n_col
    chunks = cols // LANES
    line = n_col // 2
    fine = by_slab(kb, kr, line)
    pieces = right_pieces(kb, kr, line, chunks)

    x = lax.axis_index("row")
    place = lax.axis_index("col")
    z, core = place // 2, lax.rem(place, 2)
    has_next, has_prev = z + 1 < line, z >= 1
    leads = core == 0

    def at(zz, cc):
        return {"col": zz * 2 + cc}

    def peer(d):
        return lax.rem(x + d, n_row)

    barrier = pltpu.get_barrier_semaphore()
    for d in range(1, n_row):
        pl.semaphore_signal(barrier, inc=1, device_id={"row": peer(d)}, device_id_type=MESH)

    def tell(sem):
        @pl.when(leads & has_next)
        def _():
            pl.semaphore_signal(sem, inc=1, device_id=at(z + 1, core), device_id_type=MESH)

        @pl.when(leads & has_prev)
        def _():
            pl.semaphore_signal(sem, inc=1, device_id=at(z - 1, core), device_id_type=MESH)

    tell(barrier)

    @pl.when(core == 1)
    def _():
        pl.semaphore_signal(barrier, inc=1, device_id=at(z, 0), device_id_type=MESH)

    own_right = pltpu.make_async_copy(
        right_hbm, right_f32.at[:, pl.ds(pl.multiple_of(x * kr, 8), kr), :], own_sem.at[0])
    own_right.start()
    own_left = pltpu.make_async_copy(
        left_hbm, left_f32.at[:, pl.ds(pl.multiple_of(place * kb, 8), kb), :], own_sem.at[1])
    own_left.start()

    beside = has_next.astype(jnp.int32) + has_prev.astype(jnp.int32)
    pl.semaphore_wait(barrier, n_row - 1 + jnp.where(leads, beside + 1, 0))

    def right_copy(d, q):
        j, first, count = pieces[q]
        span = pl.ds(pl.multiple_of(x * kr + first, 8), count)
        return pltpu.make_async_remote_copy(
            src_ref=right_hbm.at[:, pl.ds(first, count), pl.ds(j * LANES, LANES)],
            dst_ref=right_f32.at[:, span, pl.ds(j * LANES, LANES)],
            send_sem=right_send.at[d - 1, q],
            recv_sem=right_recv.at[d - 1, q],
            device_id={"row": peer(d)},
            device_id_type=MESH,
        )

    def left_slot(zz, cc, part):
        return left_f32.at[part, pl.ds(pl.multiple_of((zz * 2 + cc) * kb, 8), kb), :]

    def left_copy(way, zz, cc, part, target, own=False):
        return pltpu.make_async_remote_copy(
            src_ref=left_hbm.at[part] if own else left_slot(zz, cc, part),
            dst_ref=left_slot(zz, cc, part),
            send_sem=left_send.at[way, zz, part],
            recv_sem=left_recv.at[cc, zz, part],
            device_id=target,
            device_id_type=MESH,
        )

    def up(zz, part, own=False):
        return left_copy(0, zz, core, part, at(z + 1, core), own)

    def down(zz, part, own=False):
        return left_copy(1, zz, core, part, at(z - 1, core), own)

    def across(zz, part, own=False):
        return left_copy(2, zz, core, part, at(z, 1 - core), own)

    def arrived(zz, cc, part):
        left_copy(2, zz, cc, part, at(z, 1 - core)).wait_recv()

    def right_sends():
        for q in range(len(pieces)):
            for d in range(1, n_row):
                right_copy(d, q).start()

    def left_sends():
        for part in range(2):
            @pl.when(has_next)
            def _():
                up(z, part, True).start()

            @pl.when(has_prev)
            def _():
                down(z, part, True).start()
        for part in range(2):
            across(z, part, True).start()

    @pl.when(leads)
    def _():
        tell(near)
        left_sends()
        right_sends()
        pl.semaphore_wait(near, beside)
        pl.semaphore_signal(near, inc=1, device_id=at(z, 1), device_id_type=MESH)

    @pl.when(core == 1)
    def _():
        right_sends()
        pl.semaphore_wait(near, 1)
        left_sends()

    def to_weights(owner, q):
        j, first, count = pieces[q]
        for r in range(first, first + count, min(count, LANES)):
            n = min(count, LANES)
            row = pl.multiple_of(owner * kr + r, n)
            re = split(right_f32[0, pl.ds(row, n), j * LANES:(j + 1) * LANES])
            im = split(right_f32[1, pl.ds(row, n), j * LANES:(j + 1) * LANES])
            base = row + row // LANES * LANES
            above, below = pl.ds(pl.multiple_of(base, n), n), pl.ds(pl.multiple_of(base + LANES, n), n)
            for w, a, b in ((w_hi, re[0], im[0]), (w_lo, re[1], im[1])):
                w[j, above, :LANES] = a
                w[j, above, LANES:] = b
                w[j, below, :LANES] = -b
                w[j, below, LANES:] = a

    def convert(g):
        for part in range(2):
            block = left_f32[part, pl.ds(pl.multiple_of(g * LANES, LANES), LANES), :].T
            high, low = split(block)
            where = pl.ds(pl.multiple_of(g * PAIR + part * LANES, LANES), LANES)
            left_hi[:, where] = high
            left_lo[:, where] = low

    def multiply(j, first, count, add=False):
        span = pl.ds(pl.multiple_of(first, PAIR), count)
        total = three_dots(left_hi[:, span], left_lo[:, span], w_hi[j, span, :], w_lo[j, span, :])
        lanes = slice(j * LANES, (j + 1) * LANES)
        for part in range(2):
            value = total[:, part * LANES:(part + 1) * LANES]
            out_ref[part, :, lanes] = out_ref[part, :, lanes] + value if add else value

    def settle(zz):
        for part in range(2):
            arrived(zz, 1 - core, part)
        if fine:
            convert(zz)

    def settle_at(d):
        if d == 0:
            settle(z)
            return

        @pl.when(z - d >= 0)
        def _():
            settle(z - d)

        @pl.when(z + d < line)
        def _():
            settle(z + d)

    def right_arrived(q):
        for d in range(1, n_row):
            right_copy(d, q).wait_recv()
            to_weights(peer(n_row - d), q)

    def left_sent():
        for part in range(2):
            for d in range(line):
                own = d == 0

                @pl.when(z - d >= 0)
                def _():
                    @pl.when(has_next)
                    def _():
                        up(z - d, part, own).wait_send()

                    across(z - d, part, own).wait_send()

                @pl.when(z + d < line)
                def _():
                    @pl.when(has_prev)
                    def _():
                        down(z + d, part, own).wait_send()

                    if d > 0:
                        across(z + d, part).wait_send()

    own_right.wait()
    for q in range(len(pieces)):
        to_weights(x, q)
    own_left.wait()

    far = jnp.where(2 * z < line, line - 1, 0)
    others = jnp.where(2 * z < line, 0, PAIR)

    def most(j):
        right_arrived(j)
        multiply(j, others, (line - 1) * PAIR)

    early = max(chunks - 2, 0) if fine else 0
    for d in range(1, line):
        if fine and d == line - 1:
            settle_at(d - 1)
            for j in range(early):
                most(j)
        for part in range(2):
            @pl.when(z - d >= 0)
            def _():
                arrived(z - d, core, part)

                @pl.when(has_next)
                def _():
                    up(z - d, part).start()

                across(z - d, part).start()

            @pl.when(z + d < line)
            def _():
                arrived(z + d, core, part)

                @pl.when(has_prev)
                def _():
                    down(z + d, part).start()

                across(z + d, part).start()

        if not (fine and d == line - 1):
            settle_at(d - 1)

    if fine:
        for j in range(early, chunks - 1):
            most(j)
        settle_at(line - 1)
        for j in range(chunks - 1):
            multiply(j, far * PAIR, PAIR, True)
        for i in range(kr // LANES):
            multiply(chunks - 1, (x * (kr // LANES) + i) * PAIR, PAIR, i > 0)
        left_sent()
        for q in range(chunks - 1, len(pieces)):
            for d in range(1, n_row):
                owner = peer(n_row - d)
                right_copy(d, q).wait_recv()
                to_weights(owner, q)
                multiply(chunks - 1, (owner * (kr // LANES) + pieces[q][1] // LANES) * PAIR, PAIR, True)
    else:
        settle_at(line - 1)
        for g in range(depth // LANES):
            convert(g)
        left_sent()
        for j in range(chunks):
            right_arrived(j)
            multiply(j, 0, 2 * depth)

    for q in range(len(pieces)):
        for d in range(1, n_row):
            right_copy(d, q).wait_send()


def body(n_row, n_col, left_data, right_data):
    left = jnp.swapaxes(left_data, 1, 2)
    _, kb, rows = left.shape
    _, kr, cols = right_data.shape
    depth, chunks, line = kb * n_col, cols // LANES, n_col // 2
    n_pieces = len(right_pieces(kb, kr, line, chunks))
    vmem = pl.BlockSpec(memory_space=pltpu.VMEM)
    done = pl.pallas_call(
        functools.partial(kernel, n_row, n_col),
        out_shape=jax.ShapeDtypeStruct((2, rows, cols), jnp.float32),
        in_specs=[pl.BlockSpec(memory_space=pltpu.HBM)] * 2,
        out_specs=vmem,
        scratch_shapes=[
            pltpu.VMEM((rows, 2 * depth), jnp.bfloat16),
            pltpu.VMEM((rows, 2 * depth), jnp.bfloat16),
            pltpu.VMEM((chunks, 2 * depth, PAIR), jnp.bfloat16),
            pltpu.VMEM((chunks, 2 * depth, PAIR), jnp.bfloat16),
            pltpu.VMEM((2, depth, rows), jnp.float32),
            pltpu.VMEM((2, depth, cols), jnp.float32),
            pltpu.SemaphoreType.DMA((2,)),
            pltpu.SemaphoreType.REGULAR,
            pltpu.SemaphoreType.DMA((3, line, 2)),
            pltpu.SemaphoreType.DMA((2, line, 2)),
            pltpu.SemaphoreType.DMA((n_row - 1, n_pieces)),
            pltpu.SemaphoreType.DMA((n_row - 1, n_pieces)),
        ],
        compiler_params=pltpu.CompilerParams(
            collective_id=0, has_side_effects=True, vmem_limit_bytes=32 * 1024 * 1024),
    )(pltpu.with_memory_space_constraint(left, pltpu.HBM), pltpu.with_memory_space_constraint(right_data, pltpu.HBM))
    return pl.pallas_call(
        write,
        out_shape=jax.ShapeDtypeStruct((2, rows, cols), jnp.float32),
        in_specs=[vmem],
        out_specs=pl.BlockSpec(memory_space=pltpu.HBM),
        scratch_shapes=[pltpu.SemaphoreType.DMA((1,))],
        compiler_params=pltpu.CompilerParams(vmem_limit_bytes=16 * 1024 * 1024),
    )(done)


def solution(mesh):
    placed = (P(None, ("freq", "row"), "col"), P(None, "row", ("freq", "col")))
    return jax.shard_map(
        functools.partial(body, mesh.shape["row"], mesh.shape["col"]),
        mesh=mesh, in_specs=placed, out_specs=P(None, ("freq", "row"), "col"), check_vma=False,
    )
```

```python
import functools

import jax
import jax.numpy as jnp
from jax import lax
from jax.experimental import pallas as pl
from jax.experimental.pallas import tpu as pltpu
from jax.sharding import PartitionSpec as P

MESH = pl.DeviceIdType.MESH
LANES = 128
PAIR = 2 * LANES


def split(value):
    high = value.astype(jnp.bfloat16)
    return high, (value - high.astype(jnp.float32)).astype(jnp.bfloat16)


def dot(a, b):
    return jnp.dot(a, b, preferred_element_type=jnp.float32)


def three_dots(left_hi, left_lo, w_hi, w_lo):
    return dot(left_hi, w_hi) + (dot(left_hi, w_lo) + dot(left_lo, w_hi))


def by_slab(kb, kr, line):
    return 2 * kb == LANES and kr % LANES == 0 and line > 1


def right_pieces(kb, kr, line, chunks):
    pieces = [(j, 0, kr) for j in range(chunks)]
    if by_slab(kb, kr, line):
        pieces[-1:] = [(chunks - 1, r, LANES) for r in range(0, kr, LANES)]
    return pieces


def finish(
    n_row, step, done_ref, left_hi, left_lo, last_hi, last_lo, out_hbm, tail, sem,
):
    _, rows, cols = done_ref.shape
    if step is None:
        copy = pltpu.make_async_copy(done_ref, out_hbm, sem.at[0])
        copy.start()
        copy.wait()
        return
    groups, offset = step
    ready, half = cols - LANES, rows // 2
    early = pltpu.make_async_copy(
        done_ref.at[:, :, pl.ds(0, ready)], out_hbm.at[:, :, pl.ds(0, ready)], sem.at[0])
    early.start()
    copies = [early]
    x = lax.axis_index("row")
    for i in range(2):
        span = pl.ds(i * half, half)
        total = jnp.concatenate([done_ref[part, span, ready:] for part in range(2)], axis=1)
        for d in range(1, n_row):
            owner = lax.rem(x + n_row - d, n_row)
            where = pl.ds(pl.multiple_of((owner * groups + offset) * PAIR, PAIR), PAIR)
            total += three_dots(left_hi[span, where], left_lo[span, where], last_hi[d - 1], last_lo[d - 1])
        for part in range(2):
            tail[part, span, :] = total[:, part * LANES:(part + 1) * LANES]
        copy = pltpu.make_async_copy(
            tail.at[:, span, :], out_hbm.at[:, span, pl.ds(ready, LANES)], sem.at[1 + i])
        copy.start()
        copies.append(copy)
    for copy in copies:
        copy.wait()


def kernel(
    n_row, n_col, left_hbm, right_hbm, out_ref, left_hi, left_lo, last_hi, last_lo, w_hi, w_lo,
    left_f32, right_f32, own_sem, told, left_send, line_recv, pair_recv, right_send, right_recv,
):
    _, kb, rows = left_hbm.shape
    _, kr, cols = right_hbm.shape
    depth = kb * n_col
    chunks = cols // LANES
    line = n_col // 2
    fine = by_slab(kb, kr, line)
    pieces = right_pieces(kb, kr, line, chunks)

    x = lax.axis_index("row")
    place = lax.axis_index("col")
    z, core = place // 2, lax.rem(place, 2)
    has_next, has_prev = z + 1 < line, z >= 1

    def at(zz, cc):
        return {"col": zz * 2 + cc}

    def peer(d):
        return lax.rem(x + d, n_row)

    def tell(sem, device):
        pl.semaphore_signal(sem, inc=1, device_id=device, device_id_type=MESH)

    barrier = pltpu.get_barrier_semaphore()
    leads = core == 0

    @pl.when(leads & has_next)
    def _():
        tell(barrier, at(z + 1, 0))

    @pl.when(core == 1)
    def _():
        for d in range(1, n_row):
            tell(barrier, {"row": peer(d)})
        tell(barrier, at(z, 0))

    own_right = pltpu.make_async_copy(
        right_hbm, right_f32.at[:, pl.ds(pl.multiple_of(x * kr, 8), kr), :], own_sem.at[0])
    own_right.start()
    own_left = pltpu.make_async_copy(
        left_hbm, left_f32.at[:, pl.ds(pl.multiple_of(place * kb, 8), kb), :], own_sem.at[1])
    own_left.start()

    pl.semaphore_wait(barrier, jnp.where(leads, 1 + has_prev.astype(jnp.int32), n_row - 1))

    def right_copy(d, q):
        j, first, count = pieces[q]
        span = pl.ds(pl.multiple_of(x * kr + first, 8), count)
        return pltpu.make_async_remote_copy(
            src_ref=right_hbm.at[:, pl.ds(first, count), pl.ds(j * LANES, LANES)],
            dst_ref=right_f32.at[:, span, pl.ds(j * LANES, LANES)],
            send_sem=right_send.at[d - 1],
            recv_sem=right_recv.at[d - 1, q],
            device_id={"row": peer(d)},
            device_id_type=MESH,
        )

    def slab(zz, cc):
        return pl.ds(pl.multiple_of((zz * 2 + cc) * kb, 8), kb)

    def left_copy(way, zz, part, target, recv_sem, own):
        here = left_f32.at[part, slab(zz, core), :]
        return pltpu.make_async_remote_copy(
            src_ref=left_hbm.at[part] if own else here,
            dst_ref=here,
            send_sem=left_send.at[way],
            recv_sem=recv_sem,
            device_id=target,
            device_id_type=MESH,
        )

    def up(zz, part, own=False):
        return left_copy(0, zz, part, at(z + 1, core), line_recv.at[zz, part], own)

    def down(zz, part, own=False):
        return left_copy(1, zz, part, at(z - 1, core), line_recv.at[zz, part], own)

    def across(zz, part, own=False):
        return left_copy(2, zz, part, at(z, 1 - core), pair_recv.at[zz], own)

    def whole_copy(ref, send_sem, recv_sem):
        return pltpu.make_async_remote_copy(
            src_ref=ref, dst_ref=ref, send_sem=send_sem, recv_sem=recv_sem,
            device_id=at(z, 1 - core), device_id_type=MESH)

    def arrived(zz, part):
        up(zz, part).wait_recv()

    def pair_arrived(zz):
        whole_copy(left_f32.at[:, slab(zz, 1 - core), :], left_send.at[2], pair_recv.at[zz]).wait_recv()

    held = len(pieces) - 1 if fine else len(pieces)

    def right_sends(first, end):
        for q in range(first, end):
            for d in range(1, n_row):
                right_copy(d, q).start()

    def both(copy):
        for part in range(2):
            copy(z, part, True).start()

    rows_in, above, below = told.at[0], told.at[1], told.at[2]
    other, beside = above, below

    @pl.when(leads)
    def _():
        tell(other, at(z, 1))

        @pl.when(has_prev)
        def _():
            tell(above, at(z - 1, 0))
            both(down)

        both(across)

        @pl.when(has_next)
        def _():
            pl.semaphore_wait(above, 1)
            both(up)
            tell(below, at(z + 1, 0))

        pl.semaphore_wait(rows_in, 1)
        right_sends(0, len(pieces))

        @pl.when(has_prev)
        def _():
            pl.semaphore_wait(below, 1)

        tell(beside, at(z, 1))

    @pl.when(core == 1)
    def _():
        right_sends(0, held)
        pl.semaphore_wait(other, 1)
        for d in range(1, n_row):
            tell(rows_in, {"row": peer(d)})
        both(across)
        pl.semaphore_wait(rows_in, n_row - 1)
        tell(rows_in, at(z, 0))
        pl.semaphore_wait(beside, 1)

        @pl.when(has_next)
        def _():
            both(up)

        @pl.when(has_prev)
        def _():
            both(down)

    def to_weights(owner, q):
        j, first, count = pieces[q]
        for r in range(first, first + count, min(count, LANES)):
            n = min(count, LANES)
            row = pl.multiple_of(owner * kr + r, n)
            re = split(right_f32[0, pl.ds(row, n), j * LANES:(j + 1) * LANES])
            im = split(right_f32[1, pl.ds(row, n), j * LANES:(j + 1) * LANES])
            base = row + row // LANES * LANES
            above, below = pl.ds(pl.multiple_of(base, n), n), pl.ds(pl.multiple_of(base + LANES, n), n)
            for w, a, b in ((w_hi, re[0], im[0]), (w_lo, re[1], im[1])):
                w[j, above, :LANES] = a
                w[j, above, LANES:] = b
                w[j, below, :LANES] = -b
                w[j, below, LANES:] = a

    def arrived_weights(g):
        block = pl.ds(pl.multiple_of(g * LANES, LANES), LANES)
        re, im = (right_f32[part, block, cols - LANES:] for part in range(2))
        return split(jnp.concatenate([jnp.concatenate([re, im], 1), jnp.concatenate([-im, re], 1)], 0))

    def convert(g, part):
        block = left_f32[part, pl.ds(pl.multiple_of(g * LANES, LANES), LANES), :].T
        high, low = split(block)
        where = pl.ds(pl.multiple_of(g * PAIR + part * LANES, LANES), LANES)
        left_hi[:, where] = high
        left_lo[:, where] = low

    def add_to(j, total):
        lanes = slice(j * LANES, (j + 1) * LANES)
        for part in range(2):
            out_ref[part, :, lanes] += total[:, part * LANES:(part + 1) * LANES]

    def multiply(j, first, count, add=False):
        span = pl.ds(pl.multiple_of(first, PAIR), count)
        total = three_dots(left_hi[:, span], left_lo[:, span], w_hi[j, span, :], w_lo[j, span, :])
        lanes = slice(j * LANES, (j + 1) * LANES)
        for part in range(2):
            value = total[:, part * LANES:(part + 1) * LANES]
            out_ref[part, :, lanes] = out_ref[part, :, lanes] + value if add else value

    def settle(d):
        def one(zz):
            pair_arrived(zz)
            if fine:
                for part in range(2):
                    convert(zz, part)

        if d == 0:
            one(z)
            return

        @pl.when(z - d >= 0)
        def _():
            one(z - d)

        @pl.when(z + d < line)
        def _():
            one(z + d)

    def right_wait(q):
        for d in range(1, n_row):
            right_copy(d, q).wait_recv()

    def right_arrived(q, waited=False):
        for d in range(1, n_row):
            if not waited:
                right_copy(d, q).wait_recv()
            to_weights(peer(n_row - d), q)

    def all_sent():
        def slabs(n, way):
            whole_copy(left_f32.at[:, pl.ds(0, n * kb), :], left_send.at[way], pair_recv.at[0]).wait_send()

        for n in range(1, line):
            @pl.when(z + 1 == n)
            def _():
                slabs(n, 0)

            @pl.when(line - z == n)
            def _():
                slabs(n, 1)

        slabs(line, 2)
        for d in range(1, n_row):
            whole_copy(right_hbm, right_send.at[d - 1], pair_recv.at[0]).wait_send()

    own_right.wait()
    for q in range(len(pieces)):
        to_weights(x, q)
    own_left.wait()

    def pass_on(d, part):
        @pl.when(z - d >= 0)
        def _():
            arrived(z - d, part)

            @pl.when(has_next)
            def _():
                up(z - d, part).start()

            across(z - d, part).start()

        @pl.when(z + d < line)
        def _():
            arrived(z + d, part)

            @pl.when(has_prev)
            def _():
                down(z + d, part).start()

            across(z + d, part).start()

    if fine:
        low = 2 * z < line
        far = jnp.where(low, line - 1, 0)
        others = jnp.where(low, 0, PAIR)
        groups = kr // LANES
        last = chunks - 1

        def most(j, waited=False):
            right_arrived(j, waited)
            multiply(j, others, (line - 1) * PAIR)

        def own_part(is_far):
            for i in range(groups):
                g = x * groups + i

                @pl.when((g == far) == is_far)
                def _():
                    multiply(last, g * PAIR, PAIR, True)

        out_ref[:, :, last * LANES:] = jnp.zeros((2, rows, LANES), jnp.float32)
        for d in range(1, line - 1):
            for part in range(2):
                pass_on(d, part)
            settle(d - 1)
        settle(line - 2)
        early = max(last - 1, 0)
        for j in range(early):
            most(j)
        own_part(False)
        pass_on(line - 1, 0)

        @pl.when(core == 1)
        def _():
            for j in range(early, last):
                right_wait(j)
            right_sends(held, len(pieces))

        pass_on(line - 1, 1)

        @pl.when(leads)
        def _():
            for j in range(early, last):
                right_wait(j)

        for j in range(early, last):
            most(j, True)
        settle(line - 1)
        for j in range(last):
            multiply(j, far * PAIR, PAIR, True)
        own_part(True)
        for q in range(last, len(pieces) - 1):
            for d in range(1, n_row):
                owner = peer(n_row - d)
                right_copy(d, q).wait_recv()
                g = owner * groups + pieces[q][1] // LANES
                span = pl.ds(pl.multiple_of(g * PAIR, PAIR), PAIR)
                add_to(last, three_dots(left_hi[:, span], left_lo[:, span], *arrived_weights(g)))
        for d in range(1, n_row):
            right_copy(d, len(pieces) - 1).wait_recv()
            g = peer(n_row - d) * groups + pieces[-1][1] // LANES
            last_hi[d - 1], last_lo[d - 1] = arrived_weights(g)
    else:
        for d in range(1, line):
            for part in range(2):
                pass_on(d, part)
            settle(d - 1)
        settle(line - 1)
        for g in range(depth // LANES):
            for part in range(2):
                convert(g, part)
        for j in range(chunks):
            right_arrived(j)
            multiply(j, 0, 2 * depth)

    all_sent()


def body(n_row, n_col, left_data, right_data):
    left = jnp.swapaxes(left_data, 1, 2)
    _, kb, rows = left.shape
    _, kr, cols = right_data.shape
    depth, chunks, line = kb * n_col, cols // LANES, n_col // 2
    n_pieces = len(right_pieces(kb, kr, line, chunks))
    vmem = pl.BlockSpec(memory_space=pltpu.VMEM)
    fine = by_slab(kb, kr, line)
    held = pl.pallas_call(
        functools.partial(kernel, n_row, n_col),
        out_shape=[
            jax.ShapeDtypeStruct((2, rows, cols), jnp.float32),
            jax.ShapeDtypeStruct((rows, 2 * depth), jnp.bfloat16),
            jax.ShapeDtypeStruct((rows, 2 * depth), jnp.bfloat16),
            jax.ShapeDtypeStruct((n_row - 1, PAIR, PAIR), jnp.bfloat16),
            jax.ShapeDtypeStruct((n_row - 1, PAIR, PAIR), jnp.bfloat16),
        ],
        in_specs=[pl.BlockSpec(memory_space=pltpu.HBM)] * 2,
        out_specs=[vmem] * 5,
        scratch_shapes=[
            pltpu.VMEM((chunks, 2 * depth, PAIR), jnp.bfloat16),
            pltpu.VMEM((chunks, 2 * depth, PAIR), jnp.bfloat16),
            pltpu.VMEM((2, depth, rows), jnp.float32),
            pltpu.VMEM((2, depth, cols), jnp.float32),
            pltpu.SemaphoreType.DMA((2,)),
            pltpu.SemaphoreType.REGULAR((3,)),
            pltpu.SemaphoreType.DMA((3,)),
            pltpu.SemaphoreType.DMA((line, 2)),
            pltpu.SemaphoreType.DMA((line,)),
            pltpu.SemaphoreType.DMA((n_row - 1,)),
            pltpu.SemaphoreType.DMA((n_row - 1, n_pieces)),
        ],
        compiler_params=pltpu.CompilerParams(
            collective_id=0, has_side_effects=True, vmem_limit_bytes=32 * 1024 * 1024),
    )(pltpu.with_memory_space_constraint(left, pltpu.HBM), pltpu.with_memory_space_constraint(right_data, pltpu.HBM))
    return pl.pallas_call(
        functools.partial(finish, n_row, (kr // LANES, kr // LANES - 1) if fine else None),
        out_shape=jax.ShapeDtypeStruct((2, rows, cols), jnp.float32),
        in_specs=[vmem] * 5,
        out_specs=pl.BlockSpec(memory_space=pltpu.HBM),
        scratch_shapes=[pltpu.VMEM((2, rows, LANES), jnp.float32), pltpu.SemaphoreType.DMA((3,))],
        compiler_params=pltpu.CompilerParams(vmem_limit_bytes=16 * 1024 * 1024),
    )(*held)


def solution(mesh):
    placed = (P(None, ("freq", "row"), "col"), P(None, "row", ("freq", "col")))
    return jax.shard_map(
        functools.partial(body, mesh.shape["row"], mesh.shape["col"]),
        mesh=mesh, in_specs=placed, out_specs=P(None, ("freq", "row"), "col"), check_vma=False,
    )
```

```python
import functools

import jax
import jax.numpy as jnp
from jax import lax
from jax.experimental import pallas as pl
from jax.experimental.pallas import tpu as pltpu
from jax.sharding import PartitionSpec as P

MESH = pl.DeviceIdType.MESH
LANES = 128
PAIR = 2 * LANES


def split(value):
    high = value.astype(jnp.bfloat16)
    return high, (value - high.astype(jnp.float32)).astype(jnp.bfloat16)


def dot(a, b):
    return jnp.dot(a, b, preferred_element_type=jnp.float32)


def three_dots(left_hi, left_lo, w_hi, w_lo):
    return dot(left_hi, w_hi) + (dot(left_hi, w_lo) + dot(left_lo, w_hi))


def by_slab(kb, kr, line):
    return 2 * kb == LANES and kr % LANES == 0 and line > 1


def right_pieces(kb, kr, line, chunks):
    pieces = [(j, 0, kr) for j in range(chunks)]
    if by_slab(kb, kr, line):
        pieces[-1:] = [(chunks - 1, r, LANES) for r in range(0, kr, LANES)]
    return pieces


def finish(
    n_row, step, done_ref, left_hi, left_lo, last_hi, last_lo, out_hbm, tail, sem,
):
    _, rows, cols = done_ref.shape
    if step is None:
        copy = pltpu.make_async_copy(done_ref, out_hbm, sem.at[0])
        copy.start()
        copy.wait()
        return
    groups, offset = step
    ready = cols - LANES
    early = pltpu.make_async_copy(
        done_ref.at[:, :, pl.ds(0, ready)], out_hbm.at[:, :, pl.ds(0, ready)], sem.at[0])
    early.start()
    x = lax.axis_index("row")
    total = jnp.concatenate([done_ref[part, :, ready:] for part in range(2)], axis=1)
    for d in range(1, n_row):
        owner = lax.rem(x + n_row - d, n_row)
        where = pl.ds(pl.multiple_of((owner * groups + offset) * PAIR, PAIR), PAIR)
        total += three_dots(left_hi[:, where], left_lo[:, where], last_hi[d - 1], last_lo[d - 1])
    for part in range(2):
        tail[part] = total[:, part * LANES:(part + 1) * LANES]
    late = pltpu.make_async_copy(tail, out_hbm.at[:, :, pl.ds(ready, LANES)], sem.at[1])
    late.start()
    early.wait()
    late.wait()


def kernel(
    n_row, n_col, left_hbm, right_hbm, out_ref, left_hi, left_lo, last_hi, last_lo, w_hi, w_lo,
    left_f32, right_f32, own_sem, told, left_send, line_recv, pair_recv, right_send, right_recv,
):
    _, kb, rows = left_hbm.shape
    _, kr, cols = right_hbm.shape
    depth = kb * n_col
    chunks = cols // LANES
    line = n_col // 2
    fine = by_slab(kb, kr, line)
    pieces = right_pieces(kb, kr, line, chunks)

    x = lax.axis_index("row")
    place = lax.axis_index("col")
    z, core = place // 2, lax.rem(place, 2)
    has_next, has_prev = z + 1 < line, z >= 1

    def at(zz, cc):
        return {"col": zz * 2 + cc}

    def peer(d):
        return lax.rem(x + d, n_row)

    def tell(sem, device):
        pl.semaphore_signal(sem, inc=1, device_id=device, device_id_type=MESH)

    barrier = pltpu.get_barrier_semaphore()
    leads = core == 0

    @pl.when(leads & has_next)
    def _():
        tell(barrier, at(z + 1, 0))

    @pl.when(core == 1)
    def _():
        for d in range(1, n_row):
            tell(barrier, {"row": peer(d)})
        tell(barrier, at(z, 0))

    own_right = pltpu.make_async_copy(
        right_hbm, right_f32.at[:, pl.ds(pl.multiple_of(x * kr, 8), kr), :], own_sem.at[0])
    own_right.start()
    own_left = pltpu.make_async_copy(
        left_hbm, left_f32.at[:, pl.ds(pl.multiple_of(place * kb, 8), kb), :], own_sem.at[1])
    own_left.start()

    pl.semaphore_wait(barrier, jnp.where(leads, 1 + has_prev.astype(jnp.int32), n_row - 1))

    def right_copy(d, q):
        j, first, count = pieces[q]
        span = pl.ds(pl.multiple_of(x * kr + first, 8), count)
        return pltpu.make_async_remote_copy(
            src_ref=right_hbm.at[:, pl.ds(first, count), pl.ds(j * LANES, LANES)],
            dst_ref=right_f32.at[:, span, pl.ds(j * LANES, LANES)],
            send_sem=right_send.at[d - 1],
            recv_sem=right_recv.at[d - 1, q],
            device_id={"row": peer(d)},
            device_id_type=MESH,
        )

    def slab(zz, cc):
        return pl.ds(pl.multiple_of((zz * 2 + cc) * kb, 8), kb)

    def left_copy(way, zz, part, target, recv_sem, own):
        here = left_f32.at[part, slab(zz, core), :]
        return pltpu.make_async_remote_copy(
            src_ref=left_hbm.at[part] if own else here,
            dst_ref=here,
            send_sem=left_send.at[way],
            recv_sem=recv_sem,
            device_id=target,
            device_id_type=MESH,
        )

    def up(zz, part, own=False):
        return left_copy(0, zz, part, at(z + 1, core), line_recv.at[lax.rem(zz - z - 2 + 2 * line, line), part], own)

    def down(zz, part, own=False):
        return left_copy(1, zz, part, at(z - 1, core), line_recv.at[lax.rem(zz - z + line, line), part], own)

    def across(zz, part, own=False):
        return left_copy(2, zz, part, at(z, 1 - core), pair_recv.at[zz], own)

    def whole_copy(ref, send_sem, recv_sem):
        return pltpu.make_async_remote_copy(
            src_ref=ref, dst_ref=ref, send_sem=send_sem, recv_sem=recv_sem,
            device_id=at(z, 1 - core), device_id_type=MESH)

    def arrived(zz, part):
        here = left_f32.at[part, slab(zz, core), :]
        whole_copy(here, left_send.at[2], line_recv.at[lax.rem(zz - z - 1 + line, line), part]).wait_recv()

    def pair_arrived(zz):
        whole_copy(left_f32.at[:, slab(zz, 1 - core), :], left_send.at[2], pair_recv.at[zz]).wait_recv()

    held = len(pieces) - 1 if fine else len(pieces)

    def right_sends(first, end):
        for q in range(first, end):
            for d in range(1, n_row):
                right_copy(d, q).start()

    def both(copy):
        for part in range(2):
            copy(z, part, True).start()

    rows_in, above, below = told.at[0], told.at[1], told.at[2]
    other, beside = above, below

    @pl.when(leads)
    def _():
        tell(other, at(z, 1))

        @pl.when(has_prev)
        def _():
            tell(above, at(z - 1, 0))
            both(down)

        both(across)

        @pl.when(has_next)
        def _():
            pl.semaphore_wait(above, 1)
            both(up)
            tell(below, at(z + 1, 0))

        pl.semaphore_wait(rows_in, 1)
        right_sends(0, len(pieces))

        @pl.when(has_prev)
        def _():
            pl.semaphore_wait(below, 1)

        tell(beside, at(z, 1))

    @pl.when(core == 1)
    def _():
        right_sends(0, held)
        pl.semaphore_wait(other, 1)
        for d in range(1, n_row):
            tell(rows_in, {"row": peer(d)})
        both(across)
        pl.semaphore_wait(rows_in, n_row - 1)
        tell(rows_in, at(z, 0))
        pl.semaphore_wait(beside, 1)

        @pl.when(has_next)
        def _():
            both(up)

        @pl.when(has_prev)
        def _():
            both(down)

    def to_weights(owner, q):
        j, first, count = pieces[q]
        for r in range(first, first + count, min(count, LANES)):
            n = min(count, LANES)
            row = pl.multiple_of(owner * kr + r, n)
            re = split(right_f32[0, pl.ds(row, n), j * LANES:(j + 1) * LANES])
            im = split(right_f32[1, pl.ds(row, n), j * LANES:(j + 1) * LANES])
            base = row + row // LANES * LANES
            above, below = pl.ds(pl.multiple_of(base, n), n), pl.ds(pl.multiple_of(base + LANES, n), n)
            for w, a, b in ((w_hi, re[0], im[0]), (w_lo, re[1], im[1])):
                w[j, above, :LANES] = a
                w[j, above, LANES:] = b
                w[j, below, :LANES] = -b
                w[j, below, LANES:] = a

    def arrived_weights(g):
        block = pl.ds(pl.multiple_of(g * LANES, LANES), LANES)
        re, im = (right_f32[part, block, cols - LANES:] for part in range(2))
        return split(jnp.concatenate([jnp.concatenate([re, im], 1), jnp.concatenate([-im, re], 1)], 0))

    def convert(g, part):
        block = left_f32[part, pl.ds(pl.multiple_of(g * LANES, LANES), LANES), :].T
        high, low = split(block)
        where = pl.ds(pl.multiple_of(g * PAIR + part * LANES, LANES), LANES)
        left_hi[:, where] = high
        left_lo[:, where] = low

    def add_to(j, total):
        lanes = slice(j * LANES, (j + 1) * LANES)
        for part in range(2):
            out_ref[part, :, lanes] += total[:, part * LANES:(part + 1) * LANES]

    def multiply(j, first, count, add=False):
        span = pl.ds(pl.multiple_of(first, PAIR), count)
        total = three_dots(left_hi[:, span], left_lo[:, span], w_hi[j, span, :], w_lo[j, span, :])
        lanes = slice(j * LANES, (j + 1) * LANES)
        for part in range(2):
            value = total[:, part * LANES:(part + 1) * LANES]
            out_ref[part, :, lanes] = out_ref[part, :, lanes] + value if add else value

    def settle(d):
        def one(zz):
            pair_arrived(zz)
            if fine:
                for part in range(2):
                    convert(zz, part)

        if d == 0:
            one(z)
            return

        @pl.when(z - d >= 0)
        def _():
            one(z - d)

        @pl.when(z + d < line)
        def _():
            one(z + d)

    def right_wait(q):
        for d in range(1, n_row):
            right_copy(d, q).wait_recv()

    def right_arrived(q, waited=False):
        for d in range(1, n_row):
            if not waited:
                right_copy(d, q).wait_recv()
            to_weights(peer(n_row - d), q)

    def all_sent():
        def slabs(n, way):
            whole_copy(left_f32.at[:, pl.ds(0, n * kb), :], left_send.at[way], pair_recv.at[0]).wait_send()

        for n in range(1, line):
            @pl.when(z + 1 == n)
            def _():
                slabs(n, 0)

            @pl.when(line - z == n)
            def _():
                slabs(n, 1)

        slabs(line, 2)
        for d in range(1, n_row):
            whole_copy(right_hbm, right_send.at[d - 1], pair_recv.at[0]).wait_send()

    own_right.wait()
    for q in range(len(pieces)):
        to_weights(x, q)
    own_left.wait()

    def pass_on(d, part):
        @pl.when(z - d >= 0)
        def _():
            arrived(z - d, part)

            @pl.when(has_next)
            def _():
                up(z - d, part).start()

            across(z - d, part).start()

        @pl.when(z + d < line)
        def _():
            arrived(z + d, part)

            @pl.when(has_prev)
            def _():
                down(z + d, part).start()

            across(z + d, part).start()

    if fine:
        low = 2 * z < line
        far = jnp.where(low, line - 1, 0)
        others = jnp.where(low, 0, PAIR)
        groups = kr // LANES
        last = chunks - 1

        def most(j, waited=False):
            right_arrived(j, waited)
            multiply(j, others, (line - 1) * PAIR)

        def own_part(is_far):
            for i in range(groups):
                g = x * groups + i

                @pl.when((g == far) == is_far)
                def _():
                    multiply(last, g * PAIR, PAIR, True)

        out_ref[:, :, last * LANES:] = jnp.zeros((2, rows, LANES), jnp.float32)
        for d in range(1, line - 1):
            for part in range(2):
                pass_on(d, part)
            settle(d - 1)
        settle(line - 2)
        early = max(last - 1, 0)
        for j in range(early):
            most(j)
        own_part(False)
        pass_on(line - 1, 0)

        @pl.when(core == 1)
        def _():
            for j in range(early, last):
                right_wait(j)
            right_sends(held, len(pieces))

        pass_on(line - 1, 1)

        @pl.when(leads)
        def _():
            for j in range(early, last):
                right_wait(j)

        for j in range(early, last):
            most(j, True)
        settle(line - 1)
        for j in range(last):
            multiply(j, far * PAIR, PAIR, True)
        own_part(True)
        for q in range(last, len(pieces) - 1):
            for d in range(1, n_row):
                owner = peer(n_row - d)
                right_copy(d, q).wait_recv()
                g = owner * groups + pieces[q][1] // LANES
                span = pl.ds(pl.multiple_of(g * PAIR, PAIR), PAIR)
                add_to(last, three_dots(left_hi[:, span], left_lo[:, span], *arrived_weights(g)))
        for d in range(1, n_row):
            right_copy(d, len(pieces) - 1).wait_recv()
            g = peer(n_row - d) * groups + pieces[-1][1] // LANES
            last_hi[d - 1], last_lo[d - 1] = arrived_weights(g)
    else:
        for d in range(1, line):
            for part in range(2):
                pass_on(d, part)
            settle(d - 1)
        settle(line - 1)
        for g in range(depth // LANES):
            for part in range(2):
                convert(g, part)
        for j in range(chunks):
            right_arrived(j)
            multiply(j, 0, 2 * depth)

    all_sent()


def body(n_row, n_col, left_data, right_data):
    left = jnp.swapaxes(left_data, 1, 2)
    _, kb, rows = left.shape
    _, kr, cols = right_data.shape
    depth, chunks, line = kb * n_col, cols // LANES, n_col // 2
    n_pieces = len(right_pieces(kb, kr, line, chunks))
    vmem = pl.BlockSpec(memory_space=pltpu.VMEM)
    fine = by_slab(kb, kr, line)
    held = pl.pallas_call(
        functools.partial(kernel, n_row, n_col),
        out_shape=[
            jax.ShapeDtypeStruct((2, rows, cols), jnp.float32),
            jax.ShapeDtypeStruct((rows, 2 * depth), jnp.bfloat16),
            jax.ShapeDtypeStruct((rows, 2 * depth), jnp.bfloat16),
            jax.ShapeDtypeStruct((n_row - 1, PAIR, PAIR), jnp.bfloat16),
            jax.ShapeDtypeStruct((n_row - 1, PAIR, PAIR), jnp.bfloat16),
        ],
        in_specs=[pl.BlockSpec(memory_space=pltpu.HBM)] * 2,
        out_specs=[vmem] * 5,
        scratch_shapes=[
            pltpu.VMEM((chunks, 2 * depth, PAIR), jnp.bfloat16),
            pltpu.VMEM((chunks, 2 * depth, PAIR), jnp.bfloat16),
            pltpu.VMEM((2, depth, rows), jnp.float32),
            pltpu.VMEM((2, depth, cols), jnp.float32),
            pltpu.SemaphoreType.DMA((2,)),
            pltpu.SemaphoreType.REGULAR((3,)),
            pltpu.SemaphoreType.DMA((3,)),
            pltpu.SemaphoreType.DMA((line - 1, 2)),
            pltpu.SemaphoreType.DMA((line,)),
            pltpu.SemaphoreType.DMA((n_row - 1,)),
            pltpu.SemaphoreType.DMA((n_row - 1, n_pieces)),
        ],
        compiler_params=pltpu.CompilerParams(
            collective_id=0, has_side_effects=True, vmem_limit_bytes=32 * 1024 * 1024),
    )(pltpu.with_memory_space_constraint(left, pltpu.HBM), pltpu.with_memory_space_constraint(right_data, pltpu.HBM))
    return pl.pallas_call(
        functools.partial(finish, n_row, (kr // LANES, kr // LANES - 1) if fine else None),
        out_shape=jax.ShapeDtypeStruct((2, rows, cols), jnp.float32),
        in_specs=[vmem] * 5,
        out_specs=pl.BlockSpec(memory_space=pltpu.HBM),
        scratch_shapes=[pltpu.VMEM((2, rows, LANES), jnp.float32), pltpu.SemaphoreType.DMA((2,))],
        compiler_params=pltpu.CompilerParams(vmem_limit_bytes=16 * 1024 * 1024),
    )(*held)


def solution(mesh):
    placed = (P(None, ("freq", "row"), "col"), P(None, "row", ("freq", "col")))
    return jax.shard_map(
        functools.partial(body, mesh.shape["row"], mesh.shape["col"]),
        mesh=mesh, in_specs=placed, out_specs=P(None, ("freq", "row"), "col"), check_vma=False,
    )
```

```python
import functools

import jax
import jax.numpy as jnp
from jax import lax
from jax.experimental import pallas as pl
from jax.experimental.pallas import tpu as pltpu
from jax.sharding import PartitionSpec as P

MESH = pl.DeviceIdType.MESH
LANES = 128
PAIR = 2 * LANES


def split(value):
    high = value.astype(jnp.bfloat16)
    return high, (value - high.astype(jnp.float32)).astype(jnp.bfloat16)


def dot(a, b):
    return jnp.dot(a, b, preferred_element_type=jnp.float32)


def three_dots(left_hi, left_lo, w_hi, w_lo):
    return dot(left_hi, w_hi) + (dot(left_hi, w_lo) + dot(left_lo, w_hi))


def by_slab(kb, kr, line):
    return 2 * kb == LANES and kr % LANES == 0 and line > 1


def right_pieces(kb, kr, line, chunks):
    pieces = [(j, 0, kr) for j in range(chunks)]
    if by_slab(kb, kr, line):
        pieces[-1:] = [(chunks - 1, r, LANES) for r in range(0, kr, LANES)]
    return pieces


def finish(
    n_row, step, done_ref, left_hi, left_lo, last_hi, last_lo, out_hbm, tail, sem,
):
    _, rows, cols = done_ref.shape
    if step is None:
        copy = pltpu.make_async_copy(done_ref, out_hbm, sem.at[0])
        copy.start()
        copy.wait()
        return
    groups, offset = step
    ready = cols - LANES
    early = pltpu.make_async_copy(
        done_ref.at[:, :, pl.ds(0, ready)], out_hbm.at[:, :, pl.ds(0, ready)], sem.at[0])
    early.start()
    x = lax.axis_index("row")
    total = jnp.concatenate([done_ref[part, :, ready:] for part in range(2)], axis=1)
    for d in range(1, n_row):
        owner = lax.rem(x + n_row - d, n_row)
        where = pl.ds(pl.multiple_of((owner * groups + offset) * PAIR, PAIR), PAIR)
        total += three_dots(left_hi[:, where], left_lo[:, where], last_hi[d - 1], last_lo[d - 1])
    for part in range(2):
        tail[part] = total[:, part * LANES:(part + 1) * LANES]
    late = pltpu.make_async_copy(tail, out_hbm.at[:, :, pl.ds(ready, LANES)], sem.at[1])
    late.start()
    early.wait()
    late.wait()


def kernel(
    n_row, n_col, left_hbm, right_hbm, out_ref, left_hi, left_lo, last_hi, last_lo, w_hi, w_lo,
    left_f32, right_f32, own_sem, told, left_send, line_recv, pair_recv, right_send, right_recv,
):
    _, kb, rows = left_hbm.shape
    _, kr, cols = right_hbm.shape
    depth = kb * n_col
    chunks = cols // LANES
    line = n_col // 2
    fine = by_slab(kb, kr, line)
    pieces = right_pieces(kb, kr, line, chunks)

    x = lax.axis_index("row")
    place = lax.axis_index("col")
    z, core = place // 2, lax.rem(place, 2)
    has_next, has_prev = z + 1 < line, z >= 1

    def at(zz, cc):
        return {"col": zz * 2 + cc}

    def peer(d):
        return lax.rem(x + d, n_row)

    def tell(sem, device):
        pl.semaphore_signal(sem, inc=1, device_id=device, device_id_type=MESH)

    barrier = pltpu.get_barrier_semaphore()
    leads = core == 0

    @pl.when(leads & has_next)
    def _():
        tell(barrier, at(z + 1, 0))

    direct = (core == 1) | (z == 0)

    @pl.when(direct)
    def _():
        for d in range(1, n_row):
            tell(barrier, {"row": peer(d)})

    @pl.when(core == 1)
    def _():
        tell(barrier, at(z, 0))

    own_right = pltpu.make_async_copy(
        right_hbm, right_f32.at[:, pl.ds(pl.multiple_of(x * kr, 8), kr), :], own_sem.at[0])
    own_right.start()
    own_left = pltpu.make_async_copy(
        left_hbm, left_f32.at[:, pl.ds(pl.multiple_of(place * kb, 8), kb), :], own_sem.at[1])
    own_left.start()

    pl.semaphore_wait(barrier, jnp.where(direct, n_row - 1, 0) + jnp.where(leads, 1 + has_prev.astype(jnp.int32), 0))

    def right_copy(d, q):
        j, first, count = pieces[q]
        span = pl.ds(pl.multiple_of(x * kr + first, 8), count)
        return pltpu.make_async_remote_copy(
            src_ref=right_hbm.at[:, pl.ds(first, count), pl.ds(j * LANES, LANES)],
            dst_ref=right_f32.at[:, span, pl.ds(j * LANES, LANES)],
            send_sem=right_send.at[d - 1],
            recv_sem=right_recv.at[d - 1, q],
            device_id={"row": peer(d)},
            device_id_type=MESH,
        )

    def slab(zz, cc):
        return pl.ds(pl.multiple_of((zz * 2 + cc) * kb, 8), kb)

    def left_copy(way, zz, part, target, recv_sem, own):
        here = left_f32.at[part, slab(zz, core), :]
        return pltpu.make_async_remote_copy(
            src_ref=left_hbm.at[part] if own else here,
            dst_ref=here,
            send_sem=left_send.at[way],
            recv_sem=recv_sem,
            device_id=target,
            device_id_type=MESH,
        )

    def up(zz, part, own=False):
        return left_copy(0, zz, part, at(z + 1, core), line_recv.at[lax.rem(zz - z - 2 + 2 * line, line), part], own)

    def down(zz, part, own=False):
        return left_copy(1, zz, part, at(z - 1, core), line_recv.at[lax.rem(zz - z + line, line), part], own)

    def across(zz, part, own=False):
        return left_copy(2, zz, part, at(z, 1 - core), pair_recv.at[zz], own)

    def whole_copy(ref, send_sem, recv_sem):
        return pltpu.make_async_remote_copy(
            src_ref=ref, dst_ref=ref, send_sem=send_sem, recv_sem=recv_sem,
            device_id=at(z, 1 - core), device_id_type=MESH)

    def arrived(zz, part):
        here = left_f32.at[part, slab(zz, core), :]
        whole_copy(here, left_send.at[2], line_recv.at[lax.rem(zz - z - 1 + line, line), part]).wait_recv()

    def pair_arrived(zz):
        whole_copy(left_f32.at[:, slab(zz, 1 - core), :], left_send.at[2], pair_recv.at[zz]).wait_recv()

    held = 1 if fine and line > 2 else len(pieces)

    def right_sends(first, end):
        for q in range(first, end):
            for d in range(1, n_row):
                right_copy(d, q).start()

    def both(copy):
        for part in range(2):
            copy(z, part, True).start()

    rows_in, above, below = told.at[0], told.at[1], told.at[2]
    other, beside = above, below

    @pl.when(leads)
    def _():
        @pl.when(z == 0)
        def _():
            right_sends(0, len(pieces))

        tell(other, at(z, 1))

        @pl.when(has_prev)
        def _():
            tell(above, at(z - 1, 0))
            both(down)

        both(across)

        @pl.when(has_next)
        def _():
            pl.semaphore_wait(above, 1)
            both(up)
            tell(below, at(z + 1, 0))

        @pl.when(has_prev)
        def _():
            pl.semaphore_wait(rows_in, 1)
            right_sends(0, len(pieces))
            pl.semaphore_wait(below, 1)

        tell(beside, at(z, 1))

    @pl.when(core == 1)
    def _():
        right_sends(0, held)
        pl.semaphore_wait(other, 1)
        @pl.when(has_prev)
        def _():
            for d in range(1, n_row):
                tell(rows_in, {"row": peer(d)})

        both(across)

        @pl.when(has_prev)
        def _():
            pl.semaphore_wait(rows_in, n_row - 1)
            tell(rows_in, at(z, 0))

        pl.semaphore_wait(beside, 1)

        @pl.when(has_next)
        def _():
            both(up)

        @pl.when(has_prev)
        def _():
            both(down)

    def to_weights(owner, q):
        j, first, count = pieces[q]
        for r in range(first, first + count, min(count, LANES)):
            n = min(count, LANES)
            row = pl.multiple_of(owner * kr + r, n)
            re = split(right_f32[0, pl.ds(row, n), j * LANES:(j + 1) * LANES])
            im = split(right_f32[1, pl.ds(row, n), j * LANES:(j + 1) * LANES])
            base = row + row // LANES * LANES
            above, below = pl.ds(pl.multiple_of(base, n), n), pl.ds(pl.multiple_of(base + LANES, n), n)
            for w, a, b in ((w_hi, re[0], im[0]), (w_lo, re[1], im[1])):
                w[j, above, :LANES] = a
                w[j, above, LANES:] = b
                w[j, below, :LANES] = -b
                w[j, below, LANES:] = a

    def arrived_weights(g):
        block = pl.ds(pl.multiple_of(g * LANES, LANES), LANES)
        re, im = (right_f32[part, block, cols - LANES:] for part in range(2))
        return split(jnp.concatenate([jnp.concatenate([re, im], 1), jnp.concatenate([-im, re], 1)], 0))

    def convert(g, part):
        block = left_f32[part, pl.ds(pl.multiple_of(g * LANES, LANES), LANES), :].T
        high, low = split(block)
        where = pl.ds(pl.multiple_of(g * PAIR + part * LANES, LANES), LANES)
        left_hi[:, where] = high
        left_lo[:, where] = low

    def add_to(j, total):
        lanes = slice(j * LANES, (j + 1) * LANES)
        for part in range(2):
            out_ref[part, :, lanes] += total[:, part * LANES:(part + 1) * LANES]

    def multiply(j, first, count, add=False):
        span = pl.ds(pl.multiple_of(first, PAIR), count)
        total = three_dots(left_hi[:, span], left_lo[:, span], w_hi[j, span, :], w_lo[j, span, :])
        lanes = slice(j * LANES, (j + 1) * LANES)
        for part in range(2):
            value = total[:, part * LANES:(part + 1) * LANES]
            out_ref[part, :, lanes] = out_ref[part, :, lanes] + value if add else value

    def settle(d):
        def one(zz):
            pair_arrived(zz)
            if fine:
                for part in range(2):
                    convert(zz, part)

        if d == 0:
            one(z)
            return

        @pl.when(z - d >= 0)
        def _():
            one(z - d)

        @pl.when(z + d < line)
        def _():
            one(z + d)

    def right_arrived(q):
        for d in range(1, n_row):
            right_copy(d, q).wait_recv()
            to_weights(peer(n_row - d), q)

    def all_sent():
        def slabs(n, way):
            whole_copy(left_f32.at[:, pl.ds(0, n * kb), :], left_send.at[way], pair_recv.at[0]).wait_send()

        for n in range(1, line):
            @pl.when(z + 1 == n)
            def _():
                slabs(n, 0)

            @pl.when(line - z == n)
            def _():
                slabs(n, 1)

        slabs(line, 2)
        for d in range(1, n_row):
            whole_copy(right_hbm, right_send.at[d - 1], pair_recv.at[0]).wait_send()

    own_right.wait()
    for q in range(len(pieces)):
        to_weights(x, q)
    own_left.wait()

    def pass_on(d, part):
        @pl.when(z - d >= 0)
        def _():
            arrived(z - d, part)

            @pl.when(has_next)
            def _():
                up(z - d, part).start()

            across(z - d, part).start()

        @pl.when(z + d < line)
        def _():
            arrived(z + d, part)

            @pl.when(has_prev)
            def _():
                down(z + d, part).start()

            across(z + d, part).start()

    if fine:
        low = 2 * z < line
        far = jnp.where(low, line - 1, 0)
        others = jnp.where(low, 0, PAIR)
        groups = kr // LANES
        last = chunks - 1

        def most(j):
            right_arrived(j)
            multiply(j, others, (line - 1) * PAIR)

        def own_part(is_far):
            for i in range(groups):
                g = x * groups + i

                @pl.when((g == far) == is_far)
                def _():
                    multiply(last, g * PAIR, PAIR, True)

        out_ref[:, :, last * LANES:] = jnp.zeros((2, rows, LANES), jnp.float32)
        for d in range(1, line - 1):
            for part in range(2):
                pass_on(d, part)
                if d == 1 and part == 0:
                    @pl.when(core == 1)
                    def _():
                        right_sends(held, len(pieces))

            settle(d - 1)
        settle(line - 2)
        early = max(last - 1, 0)
        for j in range(early):
            most(j)
        own_part(False)
        pass_on(line - 1, 0)

        pass_on(line - 1, 1)
        for j in range(early, last):
            most(j)
        settle(line - 1)
        for j in range(last):
            multiply(j, far * PAIR, PAIR, True)
        own_part(True)
        for q in range(last, len(pieces) - 1):
            for d in range(1, n_row):
                owner = peer(n_row - d)
                right_copy(d, q).wait_recv()
                g = owner * groups + pieces[q][1] // LANES
                span = pl.ds(pl.multiple_of(g * PAIR, PAIR), PAIR)
                add_to(last, three_dots(left_hi[:, span], left_lo[:, span], *arrived_weights(g)))
        for d in range(1, n_row):
            right_copy(d, len(pieces) - 1).wait_recv()
            g = peer(n_row - d) * groups + pieces[-1][1] // LANES
            last_hi[d - 1], last_lo[d - 1] = arrived_weights(g)
    else:
        for d in range(1, line):
            for part in range(2):
                pass_on(d, part)
            settle(d - 1)
        settle(line - 1)
        for g in range(depth // LANES):
            for part in range(2):
                convert(g, part)
        for j in range(chunks):
            right_arrived(j)
            multiply(j, 0, 2 * depth)

    all_sent()


def body(n_row, n_col, left_data, right_data):
    left = jnp.swapaxes(left_data, 1, 2)
    _, kb, rows = left.shape
    _, kr, cols = right_data.shape
    depth, chunks, line = kb * n_col, cols // LANES, n_col // 2
    n_pieces = len(right_pieces(kb, kr, line, chunks))
    vmem = pl.BlockSpec(memory_space=pltpu.VMEM)
    fine = by_slab(kb, kr, line)
    held = pl.pallas_call(
        functools.partial(kernel, n_row, n_col),
        out_shape=[
            jax.ShapeDtypeStruct((2, rows, cols), jnp.float32),
            jax.ShapeDtypeStruct((rows, 2 * depth), jnp.bfloat16),
            jax.ShapeDtypeStruct((rows, 2 * depth), jnp.bfloat16),
            jax.ShapeDtypeStruct((n_row - 1, PAIR, PAIR), jnp.bfloat16),
            jax.ShapeDtypeStruct((n_row - 1, PAIR, PAIR), jnp.bfloat16),
        ],
        in_specs=[pl.BlockSpec(memory_space=pltpu.HBM)] * 2,
        out_specs=[vmem] * 5,
        scratch_shapes=[
            pltpu.VMEM((chunks, 2 * depth, PAIR), jnp.bfloat16),
            pltpu.VMEM((chunks, 2 * depth, PAIR), jnp.bfloat16),
            pltpu.VMEM((2, depth, rows), jnp.float32),
            pltpu.VMEM((2, depth, cols), jnp.float32),
            pltpu.SemaphoreType.DMA((2,)),
            pltpu.SemaphoreType.REGULAR((3,)),
            pltpu.SemaphoreType.DMA((3,)),
            pltpu.SemaphoreType.DMA((line - 1, 2)),
            pltpu.SemaphoreType.DMA((line,)),
            pltpu.SemaphoreType.DMA((n_row - 1,)),
            pltpu.SemaphoreType.DMA((n_row - 1, n_pieces)),
        ],
        compiler_params=pltpu.CompilerParams(
            collective_id=0, has_side_effects=True, vmem_limit_bytes=32 * 1024 * 1024),
    )(pltpu.with_memory_space_constraint(left, pltpu.HBM), pltpu.with_memory_space_constraint(right_data, pltpu.HBM))
    return pl.pallas_call(
        functools.partial(finish, n_row, (kr // LANES, kr // LANES - 1) if fine else None),
        out_shape=jax.ShapeDtypeStruct((2, rows, cols), jnp.float32),
        in_specs=[vmem] * 5,
        out_specs=pl.BlockSpec(memory_space=pltpu.HBM),
        scratch_shapes=[pltpu.VMEM((2, rows, LANES), jnp.float32), pltpu.SemaphoreType.DMA((2,))],
        compiler_params=pltpu.CompilerParams(vmem_limit_bytes=16 * 1024 * 1024),
    )(*held)


def solution(mesh):
    placed = (P(None, ("freq", "row"), "col"), P(None, "row", ("freq", "col")))
    return jax.shard_map(
        functools.partial(body, mesh.shape["row"], mesh.shape["col"]),
        mesh=mesh, in_specs=placed, out_specs=P(None, ("freq", "row"), "col"), check_vma=False,
    )
```

```python
import functools

import jax
import jax.numpy as jnp
from jax import lax
from jax.experimental import pallas as pl
from jax.experimental.pallas import tpu as pltpu
from jax.sharding import PartitionSpec as P

MESH = pl.DeviceIdType.MESH
LANES = 128
PAIR = 2 * LANES


def split(value):
    high = value.astype(jnp.bfloat16)
    return high, (value - high.astype(jnp.float32)).astype(jnp.bfloat16)


def dot(a, b):
    return jnp.dot(a, b, preferred_element_type=jnp.float32)


def three_dots(left_hi, left_lo, w_hi, w_lo):
    return dot(left_hi, w_hi) + (dot(left_hi, w_lo) + dot(left_lo, w_hi))


def by_slab(kb, kr, line):
    return 2 * kb == LANES and kr % LANES == 0 and line > 1


def right_pieces(kb, kr, line, chunks):
    pieces = [(j, 0, kr) for j in range(chunks)]
    if by_slab(kb, kr, line):
        pieces[-1:] = [(chunks - 1, r, LANES) for r in range(0, kr, LANES)]
    return pieces


def finish(
    n_row, step, done_ref, left_hi, left_lo, last_hi, last_lo, out_hbm, tail, sem,
):
    _, rows, cols = done_ref.shape
    if step is None:
        copy = pltpu.make_async_copy(done_ref, out_hbm, sem.at[0])
        copy.start()
        copy.wait()
        return
    groups, offset = step
    ready = cols - LANES
    early = pltpu.make_async_copy(
        done_ref.at[:, :, pl.ds(0, ready)], out_hbm.at[:, :, pl.ds(0, ready)], sem.at[0])
    early.start()
    x = lax.axis_index("row")
    total = jnp.concatenate([done_ref[part, :, ready:] for part in range(2)], axis=1)
    for d in range(1, n_row):
        owner = lax.rem(x + n_row - d, n_row)
        where = pl.ds(pl.multiple_of((owner * groups + offset) * PAIR, PAIR), PAIR)
        total += three_dots(left_hi[:, where], left_lo[:, where], last_hi[d - 1], last_lo[d - 1])
    for part in range(2):
        tail[part] = total[:, part * LANES:(part + 1) * LANES]
    late = pltpu.make_async_copy(tail, out_hbm.at[:, :, pl.ds(ready, LANES)], sem.at[1])
    late.start()
    early.wait()
    late.wait()


def kernel(
    n_row, n_col, left_hbm, right_hbm, out_ref, left_hi, left_lo, last_hi, last_lo, w_hi, w_lo,
    left_f32, right_f32, own_sem, told, left_send, line_recv, pair_recv, right_send, right_recv,
):
    _, kb, rows = left_hbm.shape
    _, kr, cols = right_hbm.shape
    depth = kb * n_col
    chunks = cols // LANES
    line = n_col // 2
    fine = by_slab(kb, kr, line)
    pieces = right_pieces(kb, kr, line, chunks)

    x = lax.axis_index("row")
    place = lax.axis_index("col")
    z, core = place // 2, lax.rem(place, 2)
    has_next, has_prev = z + 1 < line, z >= 1

    def at(zz, cc):
        return {"col": zz * 2 + cc}

    def peer(d):
        return lax.rem(x + d, n_row)

    def tell(sem, device):
        pl.semaphore_signal(sem, inc=1, device_id=device, device_id_type=MESH)

    barrier = pltpu.get_barrier_semaphore()
    leads = core == 0

    @pl.when(leads & has_next)
    def _():
        tell(barrier, at(z + 1, 0))

    direct = (core == 1) | (z == 0)

    @pl.when(direct)
    def _():
        for d in range(1, n_row):
            tell(barrier, {"row": peer(d)})

    @pl.when(core == 1)
    def _():
        tell(barrier, at(z, 0))

    own_right = pltpu.make_async_copy(
        right_hbm, right_f32.at[:, pl.ds(pl.multiple_of(x * kr, 8), kr), :], own_sem.at[0])
    own_right.start()
    own_left = pltpu.make_async_copy(
        left_hbm, left_f32.at[:, pl.ds(pl.multiple_of(place * kb, 8), kb), :], own_sem.at[1])
    own_left.start()

    pl.semaphore_wait(barrier, jnp.where(direct, n_row - 1, 0) + jnp.where(leads, 1 + has_prev.astype(jnp.int32), 0))

    paired = fine and chunks > 2

    def right_copy(d, q):
        j, first, count = pieces[q]
        span = pl.ds(pl.multiple_of(x * kr + first, 8), count)
        return pltpu.make_async_remote_copy(
            src_ref=right_hbm.at[:, pl.ds(first, count), pl.ds(j * LANES, LANES)],
            dst_ref=right_f32.at[:, span, pl.ds(j * LANES, LANES)],
            send_sem=right_send.at[d - 1],
            recv_sem=right_recv.at[d - 1, q - 1 if paired and q else q],
            device_id={"row": peer(d)},
            device_id_type=MESH,
        )

    def slab(zz, cc):
        return pl.ds(pl.multiple_of((zz * 2 + cc) * kb, 8), kb)

    def left_copy(way, zz, part, target, recv_sem, own):
        here = left_f32.at[part, slab(zz, core), :]
        return pltpu.make_async_remote_copy(
            src_ref=left_hbm.at[part] if own else here,
            dst_ref=here,
            send_sem=left_send.at[way],
            recv_sem=recv_sem,
            device_id=target,
            device_id_type=MESH,
        )

    def up(zz, part, own=False):
        return left_copy(0, zz, part, at(z + 1, core), line_recv.at[lax.rem(zz - z - 2 + 2 * line, line), part], own)

    def down(zz, part, own=False):
        return left_copy(0, zz, part, at(z - 1, core), line_recv.at[lax.rem(zz - z + line, line), part], own)

    def across(zz, part, own=False):
        return left_copy(1, zz, part, at(z, 1 - core), pair_recv.at[zz], own)

    def whole_copy(ref, send_sem, recv_sem):
        return pltpu.make_async_remote_copy(
            src_ref=ref, dst_ref=ref, send_sem=send_sem, recv_sem=recv_sem,
            device_id=at(z, 1 - core), device_id_type=MESH)

    def arrived(zz, part):
        here = left_f32.at[part, slab(zz, core), :]
        whole_copy(here, left_send.at[1], line_recv.at[lax.rem(zz - z - 1 + line, line), part]).wait_recv()

    def pair_arrived(zz):
        whole_copy(left_f32.at[:, slab(zz, 1 - core), :], left_send.at[1], pair_recv.at[zz]).wait_recv()

    held = 1 if fine and line > 2 else len(pieces)

    def right_sends(first, end):
        for q in range(first, end):
            for d in range(1, n_row):
                right_copy(d, q).start()

    def both(copy):
        for part in range(2):
            copy(z, part, True).start()

    rows_in, above, below = told.at[0], told.at[1], told.at[2]
    other, beside = above, below

    @pl.when(leads)
    def _():
        @pl.when(z == 0)
        def _():
            right_sends(0, len(pieces))

        tell(other, at(z, 1))

        @pl.when(has_prev)
        def _():
            tell(above, at(z - 1, 0))
            both(down)

        both(across)

        @pl.when(has_next)
        def _():
            pl.semaphore_wait(above, 1)
            both(up)
            tell(below, at(z + 1, 0))

        @pl.when(has_prev)
        def _():
            pl.semaphore_wait(rows_in, 1)
            right_sends(0, len(pieces))
            pl.semaphore_wait(below, 1)

        tell(beside, at(z, 1))

    @pl.when(core == 1)
    def _():
        right_sends(0, held)
        pl.semaphore_wait(other, 1)
        @pl.when(has_prev)
        def _():
            for d in range(1, n_row):
                tell(rows_in, {"row": peer(d)})

        both(across)

        @pl.when(has_prev)
        def _():
            pl.semaphore_wait(rows_in, n_row - 1)
            tell(rows_in, at(z, 0))

        pl.semaphore_wait(beside, 1)

        @pl.when(has_next)
        def _():
            both(up)

        @pl.when(has_prev)
        def _():
            both(down)

    def to_weights(owner, q):
        j, first, count = pieces[q]
        for r in range(first, first + count, min(count, LANES)):
            n = min(count, LANES)
            row = pl.multiple_of(owner * kr + r, n)
            re = split(right_f32[0, pl.ds(row, n), j * LANES:(j + 1) * LANES])
            im = split(right_f32[1, pl.ds(row, n), j * LANES:(j + 1) * LANES])
            base = row + row // LANES * LANES
            above, below = pl.ds(pl.multiple_of(base, n), n), pl.ds(pl.multiple_of(base + LANES, n), n)
            for w, a, b in ((w_hi, re[0], im[0]), (w_lo, re[1], im[1])):
                w[j, above, :LANES] = a
                w[j, above, LANES:] = b
                w[j, below, :LANES] = -b
                w[j, below, LANES:] = a

    def arrived_weights(g):
        block = pl.ds(pl.multiple_of(g * LANES, LANES), LANES)
        re, im = (right_f32[part, block, cols - LANES:] for part in range(2))
        return split(jnp.concatenate([jnp.concatenate([re, im], 1), jnp.concatenate([-im, re], 1)], 0))

    def convert(g, part):
        block = left_f32[part, pl.ds(pl.multiple_of(g * LANES, LANES), LANES), :].T
        high, low = split(block)
        where = pl.ds(pl.multiple_of(g * PAIR + part * LANES, LANES), LANES)
        left_hi[:, where] = high
        left_lo[:, where] = low

    def add_to(j, total):
        lanes = slice(j * LANES, (j + 1) * LANES)
        for part in range(2):
            out_ref[part, :, lanes] += total[:, part * LANES:(part + 1) * LANES]

    def multiply(j, first, count, add=False):
        span = pl.ds(pl.multiple_of(first, PAIR), count)
        total = three_dots(left_hi[:, span], left_lo[:, span], w_hi[j, span, :], w_lo[j, span, :])
        lanes = slice(j * LANES, (j + 1) * LANES)
        for part in range(2):
            value = total[:, part * LANES:(part + 1) * LANES]
            out_ref[part, :, lanes] = out_ref[part, :, lanes] + value if add else value

    def settle(d):
        def one(zz):
            pair_arrived(zz)
            if fine:
                for part in range(2):
                    convert(zz, part)

        if d == 0:
            one(z)
            return

        @pl.when(z - d >= 0)
        def _():
            one(z - d)

        @pl.when(z + d < line)
        def _():
            one(z + d)

    def right_arrived(q):
        for d in range(1, n_row):
            if not paired or q > 1:
                right_copy(d, q).wait_recv()
            elif q == 0:
                both_here = right_f32.at[:, pl.ds(0, kr), pl.ds(0, 2 * LANES)]
                whole_copy(both_here, left_send.at[1], right_recv.at[d - 1, 0]).wait_recv()
            to_weights(peer(n_row - d), q)

    def left_sent():
        def slabs(n, way):
            whole_copy(left_f32.at[:, pl.ds(0, n * kb), :], left_send.at[way], pair_recv.at[0]).wait_send()

        if line > 1:
            between = has_next & has_prev

            @pl.when(between)
            def _():
                slabs(line + 1, 0)

            @pl.when(~between)
            def _():
                slabs(1, 0)

        slabs(line, 1)

    def right_sent():
        for d in range(1, n_row):
            whole_copy(right_hbm, right_send.at[d - 1], pair_recv.at[0]).wait_send()

    own_right.wait()
    for q in range(len(pieces)):
        to_weights(x, q)
    own_left.wait()

    def pass_on(d, part):
        @pl.when(z - d >= 0)
        def _():
            arrived(z - d, part)

            @pl.when(has_next)
            def _():
                up(z - d, part).start()

            across(z - d, part).start()

        @pl.when(z + d < line)
        def _():
            arrived(z + d, part)

            @pl.when(has_prev)
            def _():
                down(z + d, part).start()

            across(z + d, part).start()

    if fine:
        low = 2 * z < line
        far = jnp.where(low, line - 1, 0)
        others = jnp.where(low, 0, PAIR)
        groups = kr // LANES
        last = chunks - 1

        def most(j):
            right_arrived(j)
            multiply(j, others, (line - 1) * PAIR)

        def own_part(is_far):
            for i in range(groups):
                g = x * groups + i

                @pl.when((g == far) == is_far)
                def _():
                    multiply(last, g * PAIR, PAIR, True)

        out_ref[:, :, last * LANES:] = jnp.zeros((2, rows, LANES), jnp.float32)
        for d in range(1, line - 1):
            for part in range(2):
                pass_on(d, part)
                if d == 1 and part == 0:
                    @pl.when(core == 1)
                    def _():
                        right_sends(held, len(pieces))

            settle(d - 1)
        settle(line - 2)
        early = max(last - 1, 0)
        for j in range(early):
            most(j)
        own_part(False)
        pass_on(line - 1, 0)

        pass_on(line - 1, 1)
        for j in range(early, last):
            most(j)
        settle(line - 1)
        for j in range(last):
            multiply(j, far * PAIR, PAIR, True)
        own_part(True)
        for q in range(last, len(pieces) - 1):
            for d in range(1, n_row):
                owner = peer(n_row - d)
                right_copy(d, q).wait_recv()
                g = owner * groups + pieces[q][1] // LANES
                span = pl.ds(pl.multiple_of(g * PAIR, PAIR), PAIR)
                add_to(last, three_dots(left_hi[:, span], left_lo[:, span], *arrived_weights(g)))
        left_sent()
        for d in range(1, n_row):
            right_copy(d, len(pieces) - 1).wait_recv()
            g = peer(n_row - d) * groups + pieces[-1][1] // LANES
            last_hi[d - 1], last_lo[d - 1] = arrived_weights(g)
    else:
        for d in range(1, line):
            for part in range(2):
                pass_on(d, part)
            settle(d - 1)
        settle(line - 1)
        for g in range(depth // LANES):
            for part in range(2):
                convert(g, part)
        for j in range(chunks):
            right_arrived(j)
            multiply(j, 0, 2 * depth)
        left_sent()

    right_sent()


def body(n_row, n_col, left_data, right_data):
    left = jnp.swapaxes(left_data, 1, 2)
    _, kb, rows = left.shape
    _, kr, cols = right_data.shape
    depth, chunks, line = kb * n_col, cols // LANES, n_col // 2
    n_pieces = len(right_pieces(kb, kr, line, chunks))
    vmem = pl.BlockSpec(memory_space=pltpu.VMEM)
    fine = by_slab(kb, kr, line)
    held = pl.pallas_call(
        functools.partial(kernel, n_row, n_col),
        out_shape=[
            jax.ShapeDtypeStruct((2, rows, cols), jnp.float32),
            jax.ShapeDtypeStruct((rows, 2 * depth), jnp.bfloat16),
            jax.ShapeDtypeStruct((rows, 2 * depth), jnp.bfloat16),
            jax.ShapeDtypeStruct((n_row - 1, PAIR, PAIR), jnp.bfloat16),
            jax.ShapeDtypeStruct((n_row - 1, PAIR, PAIR), jnp.bfloat16),
        ],
        in_specs=[pl.BlockSpec(memory_space=pltpu.HBM)] * 2,
        out_specs=[vmem] * 5,
        scratch_shapes=[
            pltpu.VMEM((chunks, 2 * depth, PAIR), jnp.bfloat16),
            pltpu.VMEM((chunks, 2 * depth, PAIR), jnp.bfloat16),
            pltpu.VMEM((2, depth, rows), jnp.float32),
            pltpu.VMEM((2, depth, cols), jnp.float32),
            pltpu.SemaphoreType.DMA((2,)),
            pltpu.SemaphoreType.REGULAR((3,)),
            pltpu.SemaphoreType.DMA((2,)),
            pltpu.SemaphoreType.DMA((line - 1, 2)),
            pltpu.SemaphoreType.DMA((line,)),
            pltpu.SemaphoreType.DMA((n_row - 1,)),
            pltpu.SemaphoreType.DMA((n_row - 1, n_pieces - (fine and chunks > 2))),
        ],
        compiler_params=pltpu.CompilerParams(
            collective_id=0, has_side_effects=True, vmem_limit_bytes=32 * 1024 * 1024),
    )(pltpu.with_memory_space_constraint(left, pltpu.HBM), pltpu.with_memory_space_constraint(right_data, pltpu.HBM))
    return pl.pallas_call(
        functools.partial(finish, n_row, (kr // LANES, kr // LANES - 1) if fine else None),
        out_shape=jax.ShapeDtypeStruct((2, rows, cols), jnp.float32),
        in_specs=[vmem] * 5,
        out_specs=pl.BlockSpec(memory_space=pltpu.HBM),
        scratch_shapes=[pltpu.VMEM((2, rows, LANES), jnp.float32), pltpu.SemaphoreType.DMA((2,))],
        compiler_params=pltpu.CompilerParams(vmem_limit_bytes=16 * 1024 * 1024),
    )(*held)


def solution(mesh):
    placed = (P(None, ("freq", "row"), "col"), P(None, "row", ("freq", "col")))
    return jax.shard_map(
        functools.partial(body, mesh.shape["row"], mesh.shape["col"]),
        mesh=mesh, in_specs=placed, out_specs=P(None, ("freq", "row"), "col"), check_vma=False,
    )
```

```python
import functools

import jax
import jax.numpy as jnp
from jax import lax
from jax.experimental import pallas as pl
from jax.experimental.pallas import tpu as pltpu
from jax.sharding import PartitionSpec as P

MESH = pl.DeviceIdType.MESH
LANES = 128
PAIR = 2 * LANES


def split(value):
    high = value.astype(jnp.bfloat16)
    return high, (value - high.astype(jnp.float32)).astype(jnp.bfloat16)


def dot(a, b):
    return jnp.dot(a, b, preferred_element_type=jnp.float32)


def three_dots(left_hi, left_lo, w_hi, w_lo):
    return dot(left_hi, w_hi) + (dot(left_hi, w_lo) + dot(left_lo, w_hi))


def weights(re, im):
    return split(jnp.concatenate([jnp.concatenate([re, im], 1), jnp.concatenate([-im, re], 1)], 0))


def by_slab(kb, kr, line):
    return 2 * kb == LANES and kr % LANES == 0 and line > 1


def right_pieces(kb, kr, line, chunks):
    pieces = [(j, 0, kr) for j in range(chunks)]
    if by_slab(kb, kr, line):
        pieces[-1:] = [(chunks - 1, r, LANES) for r in range(0, kr, LANES)]
    return pieces


def finish(
    n_row, step, done_ref, left_hi, left_lo, last_block, out_hbm, tail, sem,
):
    _, rows, cols = done_ref.shape
    if step is None:
        copy = pltpu.make_async_copy(done_ref, out_hbm, sem.at[0])
        copy.start()
        copy.wait()
        return
    groups, offset = step
    ready = cols - LANES
    early = pltpu.make_async_copy(
        done_ref.at[:, :, pl.ds(0, ready)], out_hbm.at[:, :, pl.ds(0, ready)], sem.at[0])
    early.start()
    x = lax.axis_index("row")
    total = jnp.concatenate([done_ref[part, :, ready:] for part in range(2)], axis=1)
    for d in range(1, n_row):
        owner = lax.rem(x + n_row - d, n_row)
        where = pl.ds(pl.multiple_of((owner * groups + offset) * PAIR, PAIR), PAIR)
        total += three_dots(
            left_hi[:, where], left_lo[:, where], *weights(last_block[d - 1, 0], last_block[d - 1, 1]))
    for part in range(2):
        tail[part] = total[:, part * LANES:(part + 1) * LANES]
    late = pltpu.make_async_copy(tail, out_hbm.at[:, :, pl.ds(ready, LANES)], sem.at[1])
    late.start()
    early.wait()
    late.wait()


def kernel(
    n_row, n_col, left_hbm, right_hbm, out_ref, left_hi, left_lo, last_block, w_hi, w_lo,
    left_f32, right_f32, own_sem, told, left_send, line_recv, pair_recv, right_send, right_recv,
):
    _, kb, rows = left_hbm.shape
    _, kr, cols = right_hbm.shape
    depth = kb * n_col
    chunks = cols // LANES
    line = n_col // 2
    fine = by_slab(kb, kr, line)
    pieces = right_pieces(kb, kr, line, chunks)

    x = lax.axis_index("row")
    place = lax.axis_index("col")
    z, core = place // 2, lax.rem(place, 2)
    has_next, has_prev = z + 1 < line, z >= 1

    def at(zz, cc):
        return {"col": zz * 2 + cc}

    def peer(d):
        return lax.rem(x + d, n_row)

    def tell(sem, device):
        pl.semaphore_signal(sem, inc=1, device_id=device, device_id_type=MESH)

    barrier = pltpu.get_barrier_semaphore()
    leads = core == 0

    @pl.when(leads & has_next)
    def _():
        tell(barrier, at(z + 1, 0))

    direct = (core == 1) | (z == 0)

    @pl.when(direct)
    def _():
        for d in range(1, n_row):
            tell(barrier, {"row": peer(d)})

    @pl.when(core == 1)
    def _():
        tell(barrier, at(z, 0))

    own_right = pltpu.make_async_copy(
        right_hbm, right_f32.at[:, pl.ds(pl.multiple_of(x * kr, 8), kr), :], own_sem.at[0])
    own_right.start()
    own_left = pltpu.make_async_copy(
        left_hbm, left_f32.at[:, pl.ds(pl.multiple_of(place * kb, 8), kb), :], own_sem.at[1])
    own_left.start()

    pl.semaphore_wait(barrier, jnp.where(direct, n_row - 1, 0) + jnp.where(leads, 1 + has_prev.astype(jnp.int32), 0))

    paired = fine and chunks > 2

    def right_copy(d, q):
        j, first, count = pieces[q]
        span = pl.ds(pl.multiple_of(x * kr + first, 8), count)
        return pltpu.make_async_remote_copy(
            src_ref=right_hbm.at[:, pl.ds(first, count), pl.ds(j * LANES, LANES)],
            dst_ref=right_f32.at[:, span, pl.ds(j * LANES, LANES)],
            send_sem=right_send.at[d - 1],
            recv_sem=right_recv.at[d - 1, q - 1 if paired and q else q],
            device_id={"row": peer(d)},
            device_id_type=MESH,
        )

    def slab(zz, cc):
        return pl.ds(pl.multiple_of((zz * 2 + cc) * kb, 8), kb)

    def left_copy(way, zz, part, target, recv_sem, own):
        here = left_f32.at[part, slab(zz, core), :]
        return pltpu.make_async_remote_copy(
            src_ref=left_hbm.at[part] if own else here,
            dst_ref=here,
            send_sem=left_send.at[way],
            recv_sem=recv_sem,
            device_id=target,
            device_id_type=MESH,
        )

    def up(zz, part, own=False):
        return left_copy(0, zz, part, at(z + 1, core), line_recv.at[lax.rem(zz - z - 2 + 2 * line, line), part], own)

    def down(zz, part, own=False):
        return left_copy(0, zz, part, at(z - 1, core), line_recv.at[lax.rem(zz - z + line, line), part], own)

    def across(zz, part, own=False):
        return left_copy(1, zz, part, at(z, 1 - core), pair_recv.at[zz], own)

    def whole_copy(ref, send_sem, recv_sem):
        return pltpu.make_async_remote_copy(
            src_ref=ref, dst_ref=ref, send_sem=send_sem, recv_sem=recv_sem,
            device_id=at(z, 1 - core), device_id_type=MESH)

    def arrived(zz, part):
        here = left_f32.at[part, slab(zz, core), :]
        whole_copy(here, left_send.at[1], line_recv.at[lax.rem(zz - z - 1 + line, line), part]).wait_recv()

    def pair_arrived(zz):
        whole_copy(left_f32.at[:, slab(zz, 1 - core), :], left_send.at[1], pair_recv.at[zz]).wait_recv()

    held = 1 if fine and line > 2 else len(pieces)

    def right_sends(first, end):
        for q in range(first, end):
            for d in range(1, n_row):
                right_copy(d, q).start()

    def both(copy):
        for part in range(2):
            copy(z, part, True).start()

    rows_in, above, below = told.at[0], told.at[1], told.at[2]
    other, beside = above, below

    @pl.when(leads)
    def _():
        @pl.when(z == 0)
        def _():
            right_sends(0, len(pieces))

        tell(other, at(z, 1))

        @pl.when(has_prev)
        def _():
            tell(above, at(z - 1, 0))
            both(down)

        both(across)

        @pl.when(has_next)
        def _():
            pl.semaphore_wait(above, 1)
            both(up)
            tell(below, at(z + 1, 0))

        @pl.when(has_prev)
        def _():
            pl.semaphore_wait(rows_in, 1)
            right_sends(0, len(pieces))
            pl.semaphore_wait(below, 1)

        tell(beside, at(z, 1))

    @pl.when(core == 1)
    def _():
        right_sends(0, held)
        pl.semaphore_wait(other, 1)
        @pl.when(has_prev)
        def _():
            for d in range(1, n_row):
                tell(rows_in, {"row": peer(d)})

        both(across)

        @pl.when(has_prev)
        def _():
            pl.semaphore_wait(rows_in, n_row - 1)
            tell(rows_in, at(z, 0))

        pl.semaphore_wait(beside, 1)

        @pl.when(has_next)
        def _():
            both(up)

        @pl.when(has_prev)
        def _():
            both(down)

    def to_weights(owner, q):
        j, first, count = pieces[q]
        for r in range(first, first + count, min(count, LANES)):
            n = min(count, LANES)
            row = pl.multiple_of(owner * kr + r, n)
            re = split(right_f32[0, pl.ds(row, n), j * LANES:(j + 1) * LANES])
            im = split(right_f32[1, pl.ds(row, n), j * LANES:(j + 1) * LANES])
            base = row + row // LANES * LANES
            above, below = pl.ds(pl.multiple_of(base, n), n), pl.ds(pl.multiple_of(base + LANES, n), n)
            for w, a, b in ((w_hi, re[0], im[0]), (w_lo, re[1], im[1])):
                w[j, above, :LANES] = a
                w[j, above, LANES:] = b
                w[j, below, :LANES] = -b
                w[j, below, LANES:] = a

    def arrived_block(g, part):
        return right_f32[part, pl.ds(pl.multiple_of(g * LANES, LANES), LANES), cols - LANES:]

    def convert(g, part):
        block = left_f32[part, pl.ds(pl.multiple_of(g * LANES, LANES), LANES), :].T
        high, low = split(block)
        where = pl.ds(pl.multiple_of(g * PAIR + part * LANES, LANES), LANES)
        left_hi[:, where] = high
        left_lo[:, where] = low

    def add_to(j, total):
        lanes = slice(j * LANES, (j + 1) * LANES)
        for part in range(2):
            out_ref[part, :, lanes] += total[:, part * LANES:(part + 1) * LANES]

    def multiply(j, first, count, add=False):
        span = pl.ds(pl.multiple_of(first, PAIR), count)
        total = three_dots(left_hi[:, span], left_lo[:, span], w_hi[j, span, :], w_lo[j, span, :])
        lanes = slice(j * LANES, (j + 1) * LANES)
        for part in range(2):
            value = total[:, part * LANES:(part + 1) * LANES]
            out_ref[part, :, lanes] = out_ref[part, :, lanes] + value if add else value

    def settle(d):
        def one(zz):
            pair_arrived(zz)
            if fine:
                for part in range(2):
                    convert(zz, part)

        if d == 0:
            one(z)
            return

        @pl.when(z - d >= 0)
        def _():
            one(z - d)

        @pl.when(z + d < line)
        def _():
            one(z + d)

    def right_arrived(q):
        for d in range(1, n_row):
            if not paired or q > 1:
                right_copy(d, q).wait_recv()
            elif q == 0:
                both_here = right_f32.at[:, pl.ds(0, kr), pl.ds(0, 2 * LANES)]
                whole_copy(both_here, left_send.at[1], right_recv.at[d - 1, 0]).wait_recv()
            to_weights(peer(n_row - d), q)

    def left_sent():
        def slabs(n, way):
            whole_copy(left_f32.at[:, pl.ds(0, n * kb), :], left_send.at[way], pair_recv.at[0]).wait_send()

        if line > 1:
            between = has_next & has_prev

            @pl.when(between)
            def _():
                slabs(line + 1, 0)

            @pl.when(~between)
            def _():
                slabs(1, 0)

        slabs(line, 1)

    def right_sent():
        for d in range(1, n_row):
            whole_copy(right_hbm, right_send.at[d - 1], pair_recv.at[0]).wait_send()

    own_right.wait()
    for q in range(len(pieces)):
        to_weights(x, q)
    own_left.wait()

    def pass_on(d, part):
        @pl.when(z - d >= 0)
        def _():
            arrived(z - d, part)

            @pl.when(has_next)
            def _():
                up(z - d, part).start()

            across(z - d, part).start()

        @pl.when(z + d < line)
        def _():
            arrived(z + d, part)

            @pl.when(has_prev)
            def _():
                down(z + d, part).start()

            across(z + d, part).start()

    if fine:
        low = 2 * z < line
        far = jnp.where(low, line - 1, 0)
        others = jnp.where(low, 0, PAIR)
        groups = kr // LANES
        last = chunks - 1

        def most(j):
            right_arrived(j)
            multiply(j, others, (line - 1) * PAIR)

        def own_part(is_far):
            for i in range(groups):
                g = x * groups + i

                @pl.when((g == far) == is_far)
                def _():
                    multiply(last, g * PAIR, PAIR, True)

        out_ref[:, :, last * LANES:] = jnp.zeros((2, rows, LANES), jnp.float32)
        for d in range(1, line - 1):
            for part in range(2):
                pass_on(d, part)
                if d == 1 and part == 0:
                    @pl.when(core == 1)
                    def _():
                        right_sends(held, len(pieces))

            settle(d - 1)
        settle(line - 2)
        early = max(last - 1, 0)
        for j in range(early):
            most(j)
        own_part(False)
        pass_on(line - 1, 0)

        pass_on(line - 1, 1)
        for j in range(early, last):
            most(j)
        settle(line - 1)
        for j in range(last):
            multiply(j, far * PAIR, PAIR, True)
        own_part(True)
        for q in range(last, len(pieces) - 1):
            for d in range(1, n_row):
                owner = peer(n_row - d)
                right_copy(d, q).wait_recv()
                g = owner * groups + pieces[q][1] // LANES
                span = pl.ds(pl.multiple_of(g * PAIR, PAIR), PAIR)
                add_to(last, three_dots(left_hi[:, span], left_lo[:, span], *weights(arrived_block(g, 0), arrived_block(g, 1))))
        left_sent()
        for d in range(1, n_row):
            right_copy(d, len(pieces) - 1).wait_recv()
            g = peer(n_row - d) * groups + pieces[-1][1] // LANES
            for part in range(2):
                last_block[d - 1, part] = arrived_block(g, part)
    else:
        for d in range(1, line):
            for part in range(2):
                pass_on(d, part)
            settle(d - 1)
        settle(line - 1)
        for g in range(depth // LANES):
            for part in range(2):
                convert(g, part)
        for j in range(chunks):
            right_arrived(j)
            multiply(j, 0, 2 * depth)
        left_sent()

    right_sent()


def body(n_row, n_col, left_data, right_data):
    left = jnp.swapaxes(left_data, 1, 2)
    _, kb, rows = left.shape
    _, kr, cols = right_data.shape
    depth, chunks, line = kb * n_col, cols // LANES, n_col // 2
    n_pieces = len(right_pieces(kb, kr, line, chunks))
    vmem = pl.BlockSpec(memory_space=pltpu.VMEM)
    fine = by_slab(kb, kr, line)
    held = pl.pallas_call(
        functools.partial(kernel, n_row, n_col),
        out_shape=[
            jax.ShapeDtypeStruct((2, rows, cols), jnp.float32),
            jax.ShapeDtypeStruct((rows, 2 * depth), jnp.bfloat16),
            jax.ShapeDtypeStruct((rows, 2 * depth), jnp.bfloat16),
            jax.ShapeDtypeStruct((n_row - 1, 2, LANES, LANES), jnp.float32),
        ],
        in_specs=[pl.BlockSpec(memory_space=pltpu.HBM)] * 2,
        out_specs=[vmem] * 4,
        scratch_shapes=[
            pltpu.VMEM((chunks, 2 * depth, PAIR), jnp.bfloat16),
            pltpu.VMEM((chunks, 2 * depth, PAIR), jnp.bfloat16),
            pltpu.VMEM((2, depth, rows), jnp.float32),
            pltpu.VMEM((2, depth, cols), jnp.float32),
            pltpu.SemaphoreType.DMA((2,)),
            pltpu.SemaphoreType.REGULAR((3,)),
            pltpu.SemaphoreType.DMA((2,)),
            pltpu.SemaphoreType.DMA((line - 1, 2)),
            pltpu.SemaphoreType.DMA((line,)),
            pltpu.SemaphoreType.DMA((n_row - 1,)),
            pltpu.SemaphoreType.DMA((n_row - 1, n_pieces - (fine and chunks > 2))),
        ],
        compiler_params=pltpu.CompilerParams(
            collective_id=0, has_side_effects=True, vmem_limit_bytes=32 * 1024 * 1024),
    )(pltpu.with_memory_space_constraint(left, pltpu.HBM), pltpu.with_memory_space_constraint(right_data, pltpu.HBM))
    return pl.pallas_call(
        functools.partial(finish, n_row, (kr // LANES, kr // LANES - 1) if fine else None),
        out_shape=jax.ShapeDtypeStruct((2, rows, cols), jnp.float32),
        in_specs=[vmem] * 4,
        out_specs=pl.BlockSpec(memory_space=pltpu.HBM),
        scratch_shapes=[pltpu.VMEM((2, rows, LANES), jnp.float32), pltpu.SemaphoreType.DMA((2,))],
        compiler_params=pltpu.CompilerParams(vmem_limit_bytes=16 * 1024 * 1024),
    )(*held)


def solution(mesh):
    placed = (P(None, ("freq", "row"), "col"), P(None, "row", ("freq", "col")))
    return jax.shard_map(
        functools.partial(body, mesh.shape["row"], mesh.shape["col"]),
        mesh=mesh, in_specs=placed, out_specs=P(None, ("freq", "row"), "col"), check_vma=False,
    )
```

```python
import functools

import jax
import jax.numpy as jnp
from jax import lax
from jax.experimental import pallas as pl
from jax.experimental.pallas import tpu as pltpu
from jax.sharding import PartitionSpec as P

MESH = pl.DeviceIdType.MESH
LANES = 128
PAIR = 2 * LANES


def split(value):
    high = value.astype(jnp.bfloat16)
    return high, (value - high.astype(jnp.float32)).astype(jnp.bfloat16)


def dot(a, b):
    return jnp.dot(a, b, preferred_element_type=jnp.float32)


def three_dots(left_hi, left_lo, w_hi, w_lo):
    return dot(left_hi, w_hi) + (dot(left_hi, w_lo) + dot(left_lo, w_hi))


def weights(re, im):
    return split(jnp.concatenate([jnp.concatenate([re, im], 1), jnp.concatenate([-im, re], 1)], 0))


def by_slab(kb, kr, line):
    return 2 * kb == LANES and kr % LANES == 0 and line > 1


def right_pieces(kb, kr, line, chunks):
    pieces = [(j, 0, kr) for j in range(chunks)]
    if by_slab(kb, kr, line):
        pieces[-1:] = [(chunks - 1, r, LANES) for r in range(0, kr, LANES)]
    return pieces


def finish(
    n_row, step, done_ref, left_hi, left_lo, last_block, out_hbm, tail, sem,
):
    _, rows, cols = done_ref.shape
    if step is None:
        copy = pltpu.make_async_copy(done_ref, out_hbm, sem.at[0])
        copy.start()
        copy.wait()
        return
    groups, offset = step
    ready = cols - LANES
    early = pltpu.make_async_copy(
        done_ref.at[:, :, pl.ds(0, ready)], out_hbm.at[:, :, pl.ds(0, ready)], sem.at[0])
    early.start()
    x = lax.axis_index("row")
    total = jnp.concatenate([done_ref[part, :, ready:] for part in range(2)], axis=1)
    for d in range(1, n_row):
        owner = lax.rem(x + n_row - d, n_row)
        where = pl.ds(pl.multiple_of((owner * groups + offset) * PAIR, PAIR), PAIR)
        total += three_dots(
            left_hi[:, where], left_lo[:, where], *weights(last_block[d - 1, 0], last_block[d - 1, 1]))
    for part in range(2):
        tail[part] = total[:, part * LANES:(part + 1) * LANES]
    late = pltpu.make_async_copy(tail, out_hbm.at[:, :, pl.ds(ready, LANES)], sem.at[1])
    late.start()
    early.wait()
    late.wait()


def kernel(
    n_row, n_col, left_hbm, right_hbm, out_ref, left_hi, left_lo, last_block, w_hi, w_lo,
    left_f32, right_f32, own_sem, told, left_send, line_recv, pair_recv, right_send, right_recv,
):
    _, kb, rows = left_hbm.shape
    _, kr, cols = right_hbm.shape
    depth = kb * n_col
    chunks = cols // LANES
    line = n_col // 2
    fine = by_slab(kb, kr, line)
    pieces = right_pieces(kb, kr, line, chunks)

    x = lax.axis_index("row")
    place = lax.axis_index("col")
    z, core = place // 2, lax.rem(place, 2)
    has_next, has_prev = z + 1 < line, z >= 1

    def at(zz, cc):
        return {"col": zz * 2 + cc}

    def peer(d):
        return lax.rem(x + d, n_row)

    def tell(sem, device):
        pl.semaphore_signal(sem, inc=1, device_id=device, device_id_type=MESH)

    barrier = pltpu.get_barrier_semaphore()
    leads = core == 0

    @pl.when(leads & has_next)
    def _():
        tell(barrier, at(z + 1, 0))

    direct = (core == 1) | (z == 0)

    @pl.when(direct)
    def _():
        for d in range(1, n_row):
            tell(barrier, {"row": peer(d)})

    @pl.when(core == 1)
    def _():
        tell(barrier, at(z, 0))

    own_right = pltpu.make_async_copy(
        right_hbm, right_f32.at[:, pl.ds(pl.multiple_of(x * kr, 8), kr), :], own_sem.at[0])
    own_left = pltpu.make_async_copy(
        left_hbm, left_f32.at[:, pl.ds(pl.multiple_of(place * kb, 8), kb), :], own_sem.at[1])

    pl.semaphore_wait(barrier, jnp.where(direct, n_row - 1, 0) + jnp.where(leads, 1 + has_prev.astype(jnp.int32), 0))

    paired = fine and chunks > 2

    def right_copy(d, q):
        j, first, count = pieces[q]
        span = pl.ds(pl.multiple_of(x * kr + first, 8), count)
        return pltpu.make_async_remote_copy(
            src_ref=right_hbm.at[:, pl.ds(first, count), pl.ds(j * LANES, LANES)],
            dst_ref=right_f32.at[:, span, pl.ds(j * LANES, LANES)],
            send_sem=right_send.at[d - 1],
            recv_sem=right_recv.at[d - 1, q - 1 if paired and q else q],
            device_id={"row": peer(d)},
            device_id_type=MESH,
        )

    def slab(zz, cc):
        return pl.ds(pl.multiple_of((zz * 2 + cc) * kb, 8), kb)

    def left_copy(way, zz, part, target, recv_sem, own):
        here = left_f32.at[part, slab(zz, core), :]
        return pltpu.make_async_remote_copy(
            src_ref=left_hbm.at[part] if own else here,
            dst_ref=here,
            send_sem=left_send.at[way],
            recv_sem=recv_sem,
            device_id=target,
            device_id_type=MESH,
        )

    def up(zz, part, own=False):
        return left_copy(0, zz, part, at(z + 1, core), line_recv.at[lax.rem(zz - z - 2 + 2 * line, line), part], own)

    def down(zz, part, own=False):
        return left_copy(0, zz, part, at(z - 1, core), line_recv.at[lax.rem(zz - z + line, line), part], own)

    def across(zz, part, own=False):
        return left_copy(1, zz, part, at(z, 1 - core), pair_recv.at[zz], own)

    def whole_copy(ref, send_sem, recv_sem):
        return pltpu.make_async_remote_copy(
            src_ref=ref, dst_ref=ref, send_sem=send_sem, recv_sem=recv_sem,
            device_id=at(z, 1 - core), device_id_type=MESH)

    def arrived(zz, part):
        here = left_f32.at[part, slab(zz, core), :]
        whole_copy(here, left_send.at[1], line_recv.at[lax.rem(zz - z - 1 + line, line), part]).wait_recv()

    def pair_arrived(zz):
        whole_copy(left_f32.at[:, slab(zz, 1 - core), :], left_send.at[1], pair_recv.at[zz]).wait_recv()

    held = 1 if fine and line > 2 else len(pieces)

    def right_sends(first, end):
        for q in range(first, end):
            for d in range(1, n_row):
                right_copy(d, q).start()

    def both(copy):
        for part in range(2):
            copy(z, part, True).start()

    rows_in, above, below = told.at[0], told.at[1], told.at[2]
    other, beside = above, below

    @pl.when(leads)
    def _():
        own_right.start()
        own_left.start()

        @pl.when(z == 0)
        def _():
            right_sends(0, len(pieces))

        tell(other, at(z, 1))

        @pl.when(has_prev)
        def _():
            tell(above, at(z - 1, 0))
            both(down)

        both(across)

        @pl.when(has_next)
        def _():
            pl.semaphore_wait(above, 1)
            both(up)
            tell(below, at(z + 1, 0))

        @pl.when(has_prev)
        def _():
            pl.semaphore_wait(rows_in, 1)
            right_sends(0, len(pieces))
            pl.semaphore_wait(below, 1)

        tell(beside, at(z, 1))

    @pl.when(core == 1)
    def _():
        right_sends(0, held)
        own_right.start()
        own_left.start()
        pl.semaphore_wait(other, 1)
        @pl.when(has_prev)
        def _():
            for d in range(1, n_row):
                tell(rows_in, {"row": peer(d)})

        both(across)

        @pl.when(has_prev)
        def _():
            pl.semaphore_wait(rows_in, n_row - 1)
            tell(rows_in, at(z, 0))

        pl.semaphore_wait(beside, 1)

        @pl.when(has_next)
        def _():
            both(up)

        @pl.when(has_prev)
        def _():
            both(down)

    def to_weights(owner, q):
        j, first, count = pieces[q]
        for r in range(first, first + count, min(count, LANES)):
            n = min(count, LANES)
            row = pl.multiple_of(owner * kr + r, n)
            re = split(right_f32[0, pl.ds(row, n), j * LANES:(j + 1) * LANES])
            im = split(right_f32[1, pl.ds(row, n), j * LANES:(j + 1) * LANES])
            base = row + row // LANES * LANES
            above, below = pl.ds(pl.multiple_of(base, n), n), pl.ds(pl.multiple_of(base + LANES, n), n)
            for w, a, b in ((w_hi, re[0], im[0]), (w_lo, re[1], im[1])):
                w[j, above, :LANES] = a
                w[j, above, LANES:] = b
                w[j, below, :LANES] = -b
                w[j, below, LANES:] = a

    def arrived_block(g, part):
        return right_f32[part, pl.ds(pl.multiple_of(g * LANES, LANES), LANES), cols - LANES:]

    def convert(g, part):
        block = left_f32[part, pl.ds(pl.multiple_of(g * LANES, LANES), LANES), :].T
        high, low = split(block)
        where = pl.ds(pl.multiple_of(g * PAIR + part * LANES, LANES), LANES)
        left_hi[:, where] = high
        left_lo[:, where] = low

    def add_to(j, total):
        lanes = slice(j * LANES, (j + 1) * LANES)
        for part in range(2):
            out_ref[part, :, lanes] += total[:, part * LANES:(part + 1) * LANES]

    def multiply(j, first, count, add=False):
        span = pl.ds(pl.multiple_of(first, PAIR), count)
        total = three_dots(left_hi[:, span], left_lo[:, span], w_hi[j, span, :], w_lo[j, span, :])
        lanes = slice(j * LANES, (j + 1) * LANES)
        for part in range(2):
            value = total[:, part * LANES:(part + 1) * LANES]
            out_ref[part, :, lanes] = out_ref[part, :, lanes] + value if add else value

    def settle(d):
        def one(zz):
            pair_arrived(zz)
            if fine:
                for part in range(2):
                    convert(zz, part)

        if d == 0:
            one(z)
            return

        @pl.when(z - d >= 0)
        def _():
            one(z - d)

        @pl.when(z + d < line)
        def _():
            one(z + d)

    def right_arrived(q):
        for d in range(1, n_row):
            if not paired or q > 1:
                right_copy(d, q).wait_recv()
            elif q == 0:
                both_here = right_f32.at[:, pl.ds(0, kr), pl.ds(0, 2 * LANES)]
                whole_copy(both_here, left_send.at[1], right_recv.at[d - 1, 0]).wait_recv()
            to_weights(peer(n_row - d), q)

    def left_sent():
        def slabs(n, way):
            whole_copy(left_f32.at[:, pl.ds(0, n * kb), :], left_send.at[way], pair_recv.at[0]).wait_send()

        if line > 1:
            between = has_next & has_prev

            @pl.when(between)
            def _():
                slabs(line + 1, 0)

            @pl.when(~between)
            def _():
                slabs(1, 0)

        slabs(line, 1)

    def right_sent():
        for d in range(1, n_row):
            whole_copy(right_hbm, right_send.at[d - 1], pair_recv.at[0]).wait_send()

    own_right.wait()
    for q in range(len(pieces)):
        to_weights(x, q)
    own_left.wait()

    def pass_on(d, part):
        @pl.when(z - d >= 0)
        def _():
            arrived(z - d, part)

            @pl.when(has_next)
            def _():
                up(z - d, part).start()

            across(z - d, part).start()

        @pl.when(z + d < line)
        def _():
            arrived(z + d, part)

            @pl.when(has_prev)
            def _():
                down(z + d, part).start()

            across(z + d, part).start()

    if fine:
        low = 2 * z < line
        far = jnp.where(low, line - 1, 0)
        others = jnp.where(low, 0, PAIR)
        groups = kr // LANES
        last = chunks - 1

        def most(j):
            right_arrived(j)
            multiply(j, others, (line - 1) * PAIR)

        def own_part(is_far):
            for i in range(groups):
                g = x * groups + i

                @pl.when((g == far) == is_far)
                def _():
                    multiply(last, g * PAIR, PAIR, True)

        out_ref[:, :, last * LANES:] = jnp.zeros((2, rows, LANES), jnp.float32)
        for d in range(1, line - 1):
            for part in range(2):
                pass_on(d, part)
                if d == 1 and part == 0:
                    @pl.when(core == 1)
                    def _():
                        right_sends(held, len(pieces))

            settle(d - 1)
        settle(line - 2)
        early = max(last - 1, 0)
        for j in range(early):
            most(j)
        own_part(False)
        pass_on(line - 1, 0)

        pass_on(line - 1, 1)
        for j in range(early, last):
            most(j)
        settle(line - 1)
        for j in range(last):
            multiply(j, far * PAIR, PAIR, True)
        own_part(True)
        for q in range(last, len(pieces) - 1):
            for d in range(1, n_row):
                owner = peer(n_row - d)
                right_copy(d, q).wait_recv()
                g = owner * groups + pieces[q][1] // LANES
                span = pl.ds(pl.multiple_of(g * PAIR, PAIR), PAIR)
                add_to(last, three_dots(left_hi[:, span], left_lo[:, span], *weights(arrived_block(g, 0), arrived_block(g, 1))))
        left_sent()
        for d in range(1, n_row):
            right_copy(d, len(pieces) - 1).wait_recv()
            g = peer(n_row - d) * groups + pieces[-1][1] // LANES
            for part in range(2):
                last_block[d - 1, part] = arrived_block(g, part)
    else:
        for d in range(1, line):
            for part in range(2):
                pass_on(d, part)
            settle(d - 1)
        settle(line - 1)
        for g in range(depth // LANES):
            for part in range(2):
                convert(g, part)
        for j in range(chunks):
            right_arrived(j)
            multiply(j, 0, 2 * depth)
        left_sent()

    right_sent()


def body(n_row, n_col, left_data, right_data):
    left = jnp.swapaxes(left_data, 1, 2)
    _, kb, rows = left.shape
    _, kr, cols = right_data.shape
    depth, chunks, line = kb * n_col, cols // LANES, n_col // 2
    n_pieces = len(right_pieces(kb, kr, line, chunks))
    vmem = pl.BlockSpec(memory_space=pltpu.VMEM)
    fine = by_slab(kb, kr, line)
    held = pl.pallas_call(
        functools.partial(kernel, n_row, n_col),
        out_shape=[
            jax.ShapeDtypeStruct((2, rows, cols), jnp.float32),
            jax.ShapeDtypeStruct((rows, 2 * depth), jnp.bfloat16),
            jax.ShapeDtypeStruct((rows, 2 * depth), jnp.bfloat16),
            jax.ShapeDtypeStruct((n_row - 1, 2, LANES, LANES), jnp.float32),
        ],
        in_specs=[pl.BlockSpec(memory_space=pltpu.HBM)] * 2,
        out_specs=[vmem] * 4,
        scratch_shapes=[
            pltpu.VMEM((chunks, 2 * depth, PAIR), jnp.bfloat16),
            pltpu.VMEM((chunks, 2 * depth, PAIR), jnp.bfloat16),
            pltpu.VMEM((2, depth, rows), jnp.float32),
            pltpu.VMEM((2, depth, cols), jnp.float32),
            pltpu.SemaphoreType.DMA((2,)),
            pltpu.SemaphoreType.REGULAR((3,)),
            pltpu.SemaphoreType.DMA((2,)),
            pltpu.SemaphoreType.DMA((line - 1, 2)),
            pltpu.SemaphoreType.DMA((line,)),
            pltpu.SemaphoreType.DMA((n_row - 1,)),
            pltpu.SemaphoreType.DMA((n_row - 1, n_pieces - (fine and chunks > 2))),
        ],
        compiler_params=pltpu.CompilerParams(
            collective_id=0, has_side_effects=True, vmem_limit_bytes=32 * 1024 * 1024),
    )(pltpu.with_memory_space_constraint(left, pltpu.HBM), pltpu.with_memory_space_constraint(right_data, pltpu.HBM))
    return pl.pallas_call(
        functools.partial(finish, n_row, (kr // LANES, kr // LANES - 1) if fine else None),
        out_shape=jax.ShapeDtypeStruct((2, rows, cols), jnp.float32),
        in_specs=[vmem] * 4,
        out_specs=pl.BlockSpec(memory_space=pltpu.HBM),
        scratch_shapes=[pltpu.VMEM((2, rows, LANES), jnp.float32), pltpu.SemaphoreType.DMA((2,))],
        compiler_params=pltpu.CompilerParams(vmem_limit_bytes=16 * 1024 * 1024),
    )(*held)


def solution(mesh):
    placed = (P(None, ("freq", "row"), "col"), P(None, "row", ("freq", "col")))
    return jax.shard_map(
        functools.partial(body, mesh.shape["row"], mesh.shape["col"]),
        mesh=mesh, in_specs=placed, out_specs=P(None, ("freq", "row"), "col"), check_vma=False,
    )
```

```python
import functools

import jax
import jax.numpy as jnp
from jax import lax
from jax.experimental import pallas as pl
from jax.experimental.pallas import tpu as pltpu
from jax.sharding import PartitionSpec as P

MESH = pl.DeviceIdType.MESH
LANES = 128
PAIR = 2 * LANES


def split(value):
    high = value.astype(jnp.bfloat16)
    return high, (value - high.astype(jnp.float32)).astype(jnp.bfloat16)


def dot(a, b):
    return jnp.dot(a, b, preferred_element_type=jnp.float32)


def three_dots(left_hi, left_lo, w_hi, w_lo):
    return dot(left_hi, w_hi) + (dot(left_hi, w_lo) + dot(left_lo, w_hi))


def weights(re, im):
    return split(jnp.concatenate([jnp.concatenate([re, im], 1), jnp.concatenate([-im, re], 1)], 0))


def by_slab(kb, kr, line):
    return 2 * kb == LANES and kr % LANES == 0 and line > 1


def right_pieces(kb, kr, line, chunks):
    pieces = [(j, 0, kr) for j in range(chunks)]
    if by_slab(kb, kr, line):
        pieces[-1:] = [(chunks - 1, r, LANES) for r in range(0, kr, LANES)]
    return pieces


def finish(
    n_row, step, done_ref, left_hi, left_lo, last_block, out_hbm, tail, sem,
):
    _, rows, cols = done_ref.shape
    if step is None:
        copy = pltpu.make_async_copy(done_ref, out_hbm, sem.at[0])
        copy.start()
        copy.wait()
        return
    groups, offset = step
    ready = cols - LANES
    early = pltpu.make_async_copy(
        done_ref.at[:, :, pl.ds(0, ready)], out_hbm.at[:, :, pl.ds(0, ready)], sem.at[0])
    early.start()
    x = lax.axis_index("row")
    total = jnp.concatenate([done_ref[part, :, ready:] for part in range(2)], axis=1)
    for d in range(1, n_row):
        owner = lax.rem(x + n_row - d, n_row)
        where = pl.ds(pl.multiple_of((owner * groups + offset) * PAIR, PAIR), PAIR)
        total += three_dots(
            left_hi[:, where], left_lo[:, where], *weights(last_block[d - 1, 0], last_block[d - 1, 1]))
    for part in range(2):
        tail[part] = total[:, part * LANES:(part + 1) * LANES]
    late = pltpu.make_async_copy(tail, out_hbm.at[:, :, pl.ds(ready, LANES)], sem.at[1])
    late.start()
    early.wait()
    late.wait()


def kernel(
    n_row, n_col, left_hbm, right_hbm, out_ref, left_hi, left_lo, last_block, w_hi, w_lo,
    left_f32, right_f32, own_sem, told, left_send, line_recv, pair_recv, right_send, right_recv,
):
    _, kb, rows = left_hbm.shape
    _, kr, cols = right_hbm.shape
    depth = kb * n_col
    chunks = cols // LANES
    line = n_col // 2
    fine = by_slab(kb, kr, line)
    pieces = right_pieces(kb, kr, line, chunks)

    x = lax.axis_index("row")
    place = lax.axis_index("col")
    z, core = place // 2, lax.rem(place, 2)
    has_next, has_prev = z + 1 < line, z >= 1

    def at(zz, cc):
        return {"col": zz * 2 + cc}

    def peer(d):
        return lax.rem(x + d, n_row)

    def tell(sem, device):
        pl.semaphore_signal(sem, inc=1, device_id=device, device_id_type=MESH)

    barrier = pltpu.get_barrier_semaphore()
    leads = core == 0

    @pl.when(leads & has_next)
    def _():
        tell(barrier, at(z + 1, 0))

    direct = (core == 1) | (z == 0)

    @pl.when(direct)
    def _():
        for d in range(1, n_row):
            tell(barrier, {"row": peer(d)})

    @pl.when(core == 1)
    def _():
        tell(barrier, at(z, 0))

    own_right = pltpu.make_async_copy(
        right_hbm, right_f32.at[:, pl.ds(pl.multiple_of(x * kr, 8), kr), :], own_sem.at[0])
    own_left = pltpu.make_async_copy(
        left_hbm, left_f32.at[:, pl.ds(pl.multiple_of(place * kb, 8), kb), :], own_sem.at[1])

    pl.semaphore_wait(barrier, jnp.where(direct, n_row - 1, 0) + jnp.where(leads, 1 + has_prev.astype(jnp.int32), 0))

    paired = fine and chunks > 2

    def right_copy(d, q):
        j, first, count = pieces[q]
        span = pl.ds(pl.multiple_of(x * kr + first, 8), count)
        return pltpu.make_async_remote_copy(
            src_ref=right_hbm.at[:, pl.ds(first, count), pl.ds(j * LANES, LANES)],
            dst_ref=right_f32.at[:, span, pl.ds(j * LANES, LANES)],
            send_sem=right_send.at[d - 1],
            recv_sem=right_recv.at[d - 1, q - 1 if paired and q else q],
            device_id={"row": peer(d)},
            device_id_type=MESH,
        )

    def slab(zz, cc):
        return pl.ds(pl.multiple_of((zz * 2 + cc) * kb, 8), kb)

    def left_copy(way, zz, part, target, recv_sem, own):
        here = left_f32.at[part, slab(zz, core), :]
        return pltpu.make_async_remote_copy(
            src_ref=left_hbm.at[part] if own else here,
            dst_ref=here,
            send_sem=left_send.at[way],
            recv_sem=recv_sem,
            device_id=target,
            device_id_type=MESH,
        )

    def up(zz, part, own=False):
        return left_copy(0, zz, part, at(z + 1, core), line_recv.at[lax.rem(zz - z - 2 + 2 * line, line), part], own)

    def down(zz, part, own=False):
        return left_copy(0, zz, part, at(z - 1, core), line_recv.at[lax.rem(zz - z + line, line), part], own)

    def across(zz, part, own=False):
        return left_copy(1, zz, part, at(z, 1 - core), pair_recv.at[zz], own)

    def whole_copy(ref, send_sem, recv_sem):
        return pltpu.make_async_remote_copy(
            src_ref=ref, dst_ref=ref, send_sem=send_sem, recv_sem=recv_sem,
            device_id=at(z, 1 - core), device_id_type=MESH)

    def arrived(zz, part):
        here = left_f32.at[part, slab(zz, core), :]
        whole_copy(here, left_send.at[1], line_recv.at[lax.rem(zz - z - 1 + line, line), part]).wait_recv()

    def pair_arrived(zz):
        whole_copy(left_f32.at[:, slab(zz, 1 - core), :], left_send.at[1], pair_recv.at[zz]).wait_recv()

    held = 1 if fine and line > 2 else len(pieces)

    def right_sends(first, end):
        for q in range(first, end):
            for d in range(1, n_row):
                right_copy(d, q).start()

    def both(copy):
        for part in range(2):
            copy(z, part, True).start()

    rows_in, above, below = told.at[0], told.at[1], told.at[2]
    other, beside = above, below

    @pl.when(leads)
    def _():
        own_right.start()
        own_left.start()

        @pl.when(z == 0)
        def _():
            right_sends(0, len(pieces))

        tell(other, at(z, 1))

        @pl.when(has_prev)
        def _():
            tell(above, at(z - 1, 0))
            both(down)

        both(across)

        @pl.when(has_next)
        def _():
            pl.semaphore_wait(above, 1)
            both(up)
            tell(below, at(z + 1, 0))

        @pl.when(has_prev)
        def _():
            pl.semaphore_wait(rows_in, 1)
            right_sends(0, len(pieces))
            pl.semaphore_wait(below, 1)

        tell(beside, at(z, 1))

    @pl.when(core == 1)
    def _():
        right_sends(0, held)
        own_right.start()
        own_left.start()
        pl.semaphore_wait(other, 1)
        @pl.when(has_prev)
        def _():
            for d in range(1, n_row):
                tell(rows_in, {"row": peer(d)})

        both(across)

        @pl.when(has_prev)
        def _():
            pl.semaphore_wait(rows_in, n_row - 1)
            tell(rows_in, at(z, 0))

        pl.semaphore_wait(beside, 1)

        @pl.when(has_next)
        def _():
            both(up)

        @pl.when(has_prev)
        def _():
            both(down)

    def to_weights(owner, q):
        j, first, count = pieces[q]
        for r in range(first, first + count, min(count, LANES)):
            n = min(count, LANES)
            row = pl.multiple_of(owner * kr + r, n)
            re = split(right_f32[0, pl.ds(row, n), j * LANES:(j + 1) * LANES])
            im = split(right_f32[1, pl.ds(row, n), j * LANES:(j + 1) * LANES])
            base = row + row // LANES * LANES
            above, below = pl.ds(pl.multiple_of(base, n), n), pl.ds(pl.multiple_of(base + LANES, n), n)
            for w, a, b in ((w_hi, re[0], im[0]), (w_lo, re[1], im[1])):
                w[j, above, :LANES] = a
                w[j, above, LANES:] = b
                w[j, below, :LANES] = -b
                w[j, below, LANES:] = a

    def arrived_block(g, part):
        return right_f32[part, pl.ds(pl.multiple_of(g * LANES, LANES), LANES), cols - LANES:]

    def convert(g, part):
        block = left_f32[part, pl.ds(pl.multiple_of(g * LANES, LANES), LANES), :].T
        high, low = split(block)
        where = pl.ds(pl.multiple_of(g * PAIR + part * LANES, LANES), LANES)
        left_hi[:, where] = high
        left_lo[:, where] = low

    def add_to(j, total):
        lanes = slice(j * LANES, (j + 1) * LANES)
        for part in range(2):
            out_ref[part, :, lanes] += total[:, part * LANES:(part + 1) * LANES]

    def multiply(j, first, count, add=False):
        span = pl.ds(pl.multiple_of(first, PAIR), count)
        total = three_dots(left_hi[:, span], left_lo[:, span], w_hi[j, span, :], w_lo[j, span, :])
        lanes = slice(j * LANES, (j + 1) * LANES)
        for part in range(2):
            value = total[:, part * LANES:(part + 1) * LANES]
            out_ref[part, :, lanes] = out_ref[part, :, lanes] + value if add else value

    def settle(d):
        def one(zz):
            pair_arrived(zz)
            if fine:
                for part in range(2):
                    convert(zz, part)

        if d == 0:
            one(z)
            return

        @pl.when(z - d >= 0)
        def _():
            one(z - d)

        @pl.when(z + d < line)
        def _():
            one(z + d)

    def right_arrived(q):
        for d in range(1, n_row):
            if not paired or q > 1:
                right_copy(d, q).wait_recv()
            elif q == 0:
                both_here = right_f32.at[:, pl.ds(0, kr), pl.ds(0, 2 * LANES)]
                whole_copy(both_here, left_send.at[1], right_recv.at[d - 1, 0]).wait_recv()
            to_weights(peer(n_row - d), q)

    def left_sent():
        def slabs(n, way):
            whole_copy(left_f32.at[:, pl.ds(0, n * kb), :], left_send.at[way], pair_recv.at[0]).wait_send()

        if line > 1:
            between = has_next & has_prev

            @pl.when(between)
            def _():
                slabs(line + 1, 0)

            @pl.when(~between)
            def _():
                slabs(1, 0)

        slabs(line, 1)

    def right_sent():
        for d in range(1, n_row):
            whole_copy(right_hbm, right_send.at[d - 1], pair_recv.at[0]).wait_send()

    own_right.wait()
    for q in range(len(pieces)):
        to_weights(x, q)
    own_left.wait()

    def pass_on(d, part):
        @pl.when(z - d >= 0)
        def _():
            arrived(z - d, part)

            @pl.when(has_next)
            def _():
                up(z - d, part).start()

            across(z - d, part).start()

        @pl.when(z + d < line)
        def _():
            arrived(z + d, part)

            @pl.when(has_prev)
            def _():
                down(z + d, part).start()

            across(z + d, part).start()

    if fine:
        low = 2 * z < line
        far = jnp.where(low, line - 1, 0)
        others = jnp.where(low, 0, PAIR)
        groups = kr // LANES
        last = chunks - 1

        def most(j):
            right_arrived(j)
            multiply(j, others, (line - 1) * PAIR)

        def own_part(is_far):
            for i in range(groups):
                g = x * groups + i

                @pl.when((g == far) == is_far)
                def _():
                    multiply(last, g * PAIR, PAIR, True)

        out_ref[:, :, last * LANES:] = jnp.zeros((2, rows, LANES), jnp.float32)
        for d in range(1, line - 1):
            for part in range(2):
                pass_on(d, part)
                if d == 1 and part == 1:
                    @pl.when(core == 1)
                    def _():
                        right_sends(held, len(pieces))

            settle(d - 1)
        settle(line - 2)
        early = max(last - 1, 0)
        for j in range(early):
            most(j)
        own_part(False)
        pass_on(line - 1, 0)

        pass_on(line - 1, 1)
        for j in range(early, last):
            most(j)
        settle(line - 1)
        for j in range(last):
            multiply(j, far * PAIR, PAIR, True)
        own_part(True)
        for q in range(last, len(pieces) - 1):
            for d in range(1, n_row):
                owner = peer(n_row - d)
                right_copy(d, q).wait_recv()
                g = owner * groups + pieces[q][1] // LANES
                span = pl.ds(pl.multiple_of(g * PAIR, PAIR), PAIR)
                add_to(last, three_dots(left_hi[:, span], left_lo[:, span], *weights(arrived_block(g, 0), arrived_block(g, 1))))
        left_sent()
        for d in range(1, n_row):
            right_copy(d, len(pieces) - 1).wait_recv()
            g = peer(n_row - d) * groups + pieces[-1][1] // LANES
            for part in range(2):
                last_block[d - 1, part] = arrived_block(g, part)
    else:
        for d in range(1, line):
            for part in range(2):
                pass_on(d, part)
            settle(d - 1)
        settle(line - 1)
        for g in range(depth // LANES):
            for part in range(2):
                convert(g, part)
        for j in range(chunks):
            right_arrived(j)
            multiply(j, 0, 2 * depth)
        left_sent()

    right_sent()


def body(n_row, n_col, left_data, right_data):
    left = jnp.swapaxes(left_data, 1, 2)
    _, kb, rows = left.shape
    _, kr, cols = right_data.shape
    depth, chunks, line = kb * n_col, cols // LANES, n_col // 2
    n_pieces = len(right_pieces(kb, kr, line, chunks))
    vmem = pl.BlockSpec(memory_space=pltpu.VMEM)
    fine = by_slab(kb, kr, line)
    held = pl.pallas_call(
        functools.partial(kernel, n_row, n_col),
        out_shape=[
            jax.ShapeDtypeStruct((2, rows, cols), jnp.float32),
            jax.ShapeDtypeStruct((rows, 2 * depth), jnp.bfloat16),
            jax.ShapeDtypeStruct((rows, 2 * depth), jnp.bfloat16),
            jax.ShapeDtypeStruct((n_row - 1, 2, LANES, LANES), jnp.float32),
        ],
        in_specs=[pl.BlockSpec(memory_space=pltpu.HBM)] * 2,
        out_specs=[vmem] * 4,
        scratch_shapes=[
            pltpu.VMEM((chunks, 2 * depth, PAIR), jnp.bfloat16),
            pltpu.VMEM((chunks, 2 * depth, PAIR), jnp.bfloat16),
            pltpu.VMEM((2, depth, rows), jnp.float32),
            pltpu.VMEM((2, depth, cols), jnp.float32),
            pltpu.SemaphoreType.DMA((2,)),
            pltpu.SemaphoreType.REGULAR((3,)),
            pltpu.SemaphoreType.DMA((2,)),
            pltpu.SemaphoreType.DMA((line - 1, 2)),
            pltpu.SemaphoreType.DMA((line,)),
            pltpu.SemaphoreType.DMA((n_row - 1,)),
            pltpu.SemaphoreType.DMA((n_row - 1, n_pieces - (fine and chunks > 2))),
        ],
        compiler_params=pltpu.CompilerParams(
            collective_id=0, has_side_effects=True, vmem_limit_bytes=32 * 1024 * 1024),
    )(pltpu.with_memory_space_constraint(left, pltpu.HBM), pltpu.with_memory_space_constraint(right_data, pltpu.HBM))
    return pl.pallas_call(
        functools.partial(finish, n_row, (kr // LANES, kr // LANES - 1) if fine else None),
        out_shape=jax.ShapeDtypeStruct((2, rows, cols), jnp.float32),
        in_specs=[vmem] * 4,
        out_specs=pl.BlockSpec(memory_space=pltpu.HBM),
        scratch_shapes=[pltpu.VMEM((2, rows, LANES), jnp.float32), pltpu.SemaphoreType.DMA((2,))],
        compiler_params=pltpu.CompilerParams(vmem_limit_bytes=16 * 1024 * 1024),
    )(*held)


def solution(mesh):
    placed = (P(None, ("freq", "row"), "col"), P(None, "row", ("freq", "col")))
    return jax.shard_map(
        functools.partial(body, mesh.shape["row"], mesh.shape["col"]),
        mesh=mesh, in_specs=placed, out_specs=P(None, ("freq", "row"), "col"), check_vma=False,
    )
```
